256 devices in a mesh: ctx: 32 (over y, x, core), tp: 8 (over z).
Axes of the slice: x: 4, y: 4, z: 8, core: 2. Of those that a mesh axis runs over, the one named last changes fastest.
Arguments:
- hyena_gate: bfloat16 [4096, 4096], P('ctx', 'tp'), may hold values from -6 to 6
- hyena_key: bfloat16 [4096, 4096], P('ctx', 'tp'), may hold values from -6 to 6
- hyena_value: bfloat16 [4096, 4096], P('ctx', 'tp'), may hold values from -6 to 6
- filter_taps: bfloat16 [4096, 4096], P(None, 'tp'), may hold values from -0.25 to 0.25
- skip_weight: float32 [4096], P('tp'), may hold values from -4 to 4
- queries: bfloat16 [4096, 4096], P('ctx', 'tp'), may hold values from -100 to 100
- attn_keys: bfloat16 [4096, 4096], P('ctx', 'tp'), may hold values from -4.5 to 4.5
- valid_length: int32 [1], replicated, may hold values from 3585 to 4096
Outputs:
- hyena_out: bfloat16 [4096, 4096], P('ctx', 'tp')
- attn_out: bfloat16 [4096, 4096], P('ctx', 'tp')
The draws below stay inside these ranges and needn't reach their ends.
All inputs are finite; a program needn't handle non-finite values.
Results may differ from the reference program's by a relative error of at most 0.015.
Values may be sent and summed in bfloat16 or wider, within the bound.
No kernel may reach another device: no remote copies, remote signals or barrier semaphores. Data moves between devices by JAX's collectives and lax.ppermute only.
A program may use at most 64 MiB of HBM per device.

```python
import math
import jax
import jax.numpy as jnp
from jax import lax

GROUP = 128
HEADS = 32
HD = 128
DW = 4096
SEQ = 4096


def key_rows(key):
    key_base = jnp.clip(jax.random.normal(jax.random.fold_in(key, 11), (SEQ, DW), jnp.float32), -4.5, 4.5)
    return key_base


def draw_attn_keys(key, part):
    key_base = key_rows(key)
    return key_base.astype(jnp.bfloat16)


def draw_queries(key, part):
    query_rows = jnp.clip(jax.random.normal(jax.random.fold_in(key, 12), (SEQ, DW), jnp.float32), -4.5, 4.5)
    return query_rows.astype(jnp.bfloat16)


def draw_filter_taps(key, part):
    channel = jnp.arange(DW, dtype=jnp.float32)
    spread = jnp.exp(jax.random.uniform(jax.random.fold_in(key, 21), (DW,), jnp.float32, math.log(0.25), math.log(2.5)))
    channel_ramp = jnp.sqrt(1.0 + 2.0 * channel / (DW - 1))
    taps_noise = jnp.clip(jax.random.normal(jax.random.fold_in(key, 22), (SEQ, DW), jnp.float32), -4.0, 4.0)
    filter_values = jnp.clip(taps_noise * (spread * channel_ramp)[None, :] / 64.0, -0.25, 0.25)
    return filter_values.astype(jnp.bfloat16)


def shard_levels(own_key, dims, pieces, low, largest):
    def one(dim, blocks):
        heights = jax.random.uniform(jax.random.fold_in(jax.random.fold_in(own_key, 6), dim), (blocks,), jnp.float32, low / len(pieces), largest / len(pieces))
        return jnp.repeat(jnp.exp(heights), dims[dim] // blocks).reshape((-1,) + (1,) * (len(dims) - dim - 1))

    gain = one(*pieces[0])
    for cut in pieces[1:]:
        gain = gain * one(*cut)
    return gain


def bell_draw(rng, dims, width, most, pieces=(), kind=jnp.bfloat16):
    values = jax.random.normal(rng, dims, jnp.float32) * width
    if len(pieces) > 0:
        values = shard_levels(rng, dims, pieces, -0.22, 0.18) * values
    return jnp.clip(values, min=-most, max=most).astype(kind)


def setup_inputs(seed: int = 0) -> dict:
    seeds = jax.random.split(jax.random.key(seed), 9)
    hyena_gate = bell_draw(seeds[0], (SEQ, DW), 1.0, 6.0, ((0, 32), (1, 8)))
    hyena_key = bell_draw(seeds[1], (SEQ, DW), 1.0, 6.0, ((0, 32), (1, 8)))
    hyena_value = bell_draw(seeds[2], (SEQ, DW), 1.0, 6.0, ((0, 32), (1, 8)))
    filter_taps = draw_filter_taps(jax.random.fold_in(seeds[8], 71), 0)
    skip_weight = bell_draw(seeds[4], (DW,), 1.0, 4.0, ((0, 8),), jnp.float32)
    queries = draw_queries(jax.random.fold_in(seeds[8], 71), 0)
    attn_keys = draw_attn_keys(jax.random.fold_in(seeds[8], 71), 0)
    valid_length = jax.random.randint(seeds[7], (1,), SEQ - 4 * GROUP + 1, SEQ + 1).astype(jnp.int32)
    return {"hyena_gate": hyena_gate, "hyena_key": hyena_key, "hyena_value": hyena_value, "filter_taps": filter_taps, "skip_weight": skip_weight, "queries": queries, "attn_keys": attn_keys, "valid_length": valid_length}


def reference(hyena_gate, hyena_key, hyena_value, filter_taps, skip_weight, queries, attn_keys, valid_length):
    mixed = (hyena_key.astype(jnp.float32) * hyena_value.astype(jnp.float32)).astype(jnp.bfloat16)
    mixed_float = mixed.astype(jnp.float32)
    doubled = 2 * SEQ
    spectrum = jnp.fft.rfft(mixed_float, n=doubled, axis=0) * jnp.fft.rfft(filter_taps.astype(jnp.float32), n=doubled, axis=0)
    convolved = jnp.fft.irfft(spectrum, n=doubled, axis=0)[:SEQ].astype(jnp.float32)
    positions = jnp.arange(SEQ, dtype=jnp.int32)
    valid_rows = positions < valid_length[0]
    gated = hyena_gate.astype(jnp.float32) * (convolved + skip_weight[None, :] * mixed_float)
    hyena_out = jnp.where(valid_rows[:, None], gated, 0.0).astype(jnp.bfloat16)
    allowed = (positions[None, :] <= positions[:, None]) & valid_rows[None, :]
    scale = 1.0 / math.sqrt(HD)

    def one_head(head):
        first = (head * HD).astype(jnp.int32)
        head_queries = lax.dynamic_slice_in_dim(queries, first, HD, 1)
        head_keys = lax.dynamic_slice_in_dim(attn_keys, first, HD, 1)
        head_values = lax.dynamic_slice_in_dim(hyena_out, first, HD, 1)
        score = jnp.dot(head_queries, head_keys.T, preferred_element_type=jnp.float32) * scale
        score = jnp.where(allowed, score, -1e+30)
        row_max = lax.optimization_barrier(jnp.max(score, axis=1, keepdims=True))
        raw = jnp.where(allowed, jnp.exp(score - row_max), 0.0)
        totals = lax.optimization_barrier(jnp.sum(raw, axis=1, keepdims=True))
        weights = raw.astype(jnp.bfloat16)
        return jnp.dot(weights, head_values, preferred_element_type=jnp.float32) / totals
    per_head = lax.map(one_head, jnp.arange(HEADS, dtype=jnp.int32))
    attended = jnp.transpose(per_head, (1, 0, 2)).reshape(SEQ, HEADS * HD)
    norm = jnp.sqrt(lax.optimization_barrier(jnp.mean(attended * attended, axis=1, keepdims=True)) + 1e-06)
    attn_out = jnp.where(valid_rows[:, None], attended / norm, 0.0).astype(jnp.bfloat16)
    return (hyena_out, attn_out)
```

```python
import functools
import math

import jax
import jax.numpy as jnp
import numpy as np
from jax import lax
from jax.experimental import pallas as pl
from jax.experimental.pallas import tpu as pltpu
from jax.sharding import PartitionSpec as P

HD = 128
DW = 4096
SEQ = 4096
G = 128
NB = SEQ // G
CH = 16
DELTA = 0.25

COLS = [[8 * y + 2 * x + e for y in range(4) for e in range(2)] for x in range(4)]
ROWS = [[8 * y + 2 * k + e for k in range(4)] for y in range(4) for e in range(2)]
COLS_TP = [[i * 8 + t for i in col for t in range(8)] for col in COLS]
CORES = [(i, i ^ 1) for i in range(32)]

BF = jnp.bfloat16
F32 = jnp.float32
NT = (((1,), (1,)), ((), ()))


def tables():
    b = np.arange(G)
    ang = 2.0 * np.pi * np.outer(b, b) / G
    c, s = np.cos(ang), np.sin(ang)
    fwd = np.block([[c, -s], [s, c]]).astype(np.float32)
    high = fwd.astype(jnp.bfloat16)
    low = (fwd - high.astype(np.float32)).astype(jnp.bfloat16)
    phase = 2.0 * np.pi * np.outer(np.arange(NB) + DELTA, b) / SEQ
    twiddle = np.stack([np.cos(phase), np.sin(phase)]).astype(np.float32)
    return high, low, high.T.copy(), low.T.copy(), twiddle


def cmul_const(z, ang):
    re, im = z
    c, s = math.cos(ang), math.sin(ang)
    if im is None:
        return (re * c, re * s) if abs(s) > 1e-12 else (re, jnp.zeros_like(re))
    if abs(s) < 1e-12:
        return (re, im) if c > 0 else (-re, -im)
    if abs(c) < 1e-12:
        return (-im, re) if s > 0 else (im, -re)
    return (re * c - im * s, re * s + im * c)


def fft(z, sign):
    n = len(z)
    if n == 1:
        return z
    half = n // 2
    up, down = [], []
    for j in range(half):
        (ar, ai), (br, bi) = z[j], z[j + half]
        up.append((ar + br, ai + bi))
        down.append(cmul_const((ar - br, ai - bi), sign * 2.0 * math.pi * j / n))
    even, odd = fft(up, sign), fft(down, sign)
    out = []
    for e, o in zip(even, odd):
        out += [e, o]
    return out


def split(x):
    high = x.astype(BF)
    return high, (x - high.astype(F32)).astype(BF)


def dot3(x, m_high, m_low):
    high, low = split(x)
    return (
        jnp.dot(high, m_high, preferred_element_type=F32)
        + jnp.dot(low, m_high, preferred_element_type=F32)
        + jnp.dot(high, m_low, preferred_element_type=F32)
    )


def spectrum(blocks, tw_ref, mh_ref, ml_ref, buf):
    z = [cmul_const((x, None), -2.0 * math.pi * DELTA * i / NB) for i, x in enumerate(blocks)]
    z = fft(z, -1.0)
    for p, (re, im) in enumerate(z):
        c, s = tw_ref[0, p : p + 1, :], tw_ref[1, p : p + 1, :]
        buf[p * CH : (p + 1) * CH, :G] = re * c + im * s
        buf[p * CH : (p + 1) * CH, G:] = im * c - re * s
    return dot3(buf[...], mh_ref[...], ml_ref[...])


def pre_kernel(key_ref, value_ref, gate_ref, attn_ref, query_ref, msg_ref, qmsg_ref):
    for h in range(4):
        cols = slice(h * HD, (h + 1) * HD)
        mixed = (key_ref[:, cols].astype(F32) * value_ref[:, cols].astype(F32)).T.astype(BF)
        gate = gate_ref[:, cols].astype(F32).T.astype(BF)
        for c in range(2):
            for k in range(4):
                e = 8 * h + 2 * k + c
                rows = slice(c * 64 + k * CH, c * 64 + (k + 1) * CH)
                msg_ref[e, 0:64, :] = attn_ref[c * 64 : (c + 1) * 64, cols]
                msg_ref[e, 64:80, :] = mixed[rows]
                msg_ref[e, 80:96, :] = gate[rows]
            qmsg_ref[2 * h + c] = query_ref[:, cols]


def taps_kernel(idx_ref, taps_ref, tw_ref, mh_ref, ml_ref, out_ref, buf):
    first = idx_ref[1]
    row = lax.broadcasted_iota(jnp.int32, (CH, G), 0)
    lane = lax.broadcasted_iota(jnp.int32, (CH, G), 1)
    pick = jnp.where(lane == row + first, 1.0, 0.0).astype(BF)
    blocks = [
        lax.dot_general(pick, taps_ref[i * G : (i + 1) * G, :], NT, preferred_element_type=F32)
        for i in range(NB)
    ]
    out_ref[...] = spectrum(blocks, tw_ref, mh_ref, ml_ref, buf)


def conv_kernel(
    idx_ref, in_ref, spec_ref, skip_ref, tw_ref, mh_ref, ml_ref, nh_ref, nl_ref, out_ref, buf
):
    valid = idx_ref[2]
    blocks = [in_ref[i, 0:CH, :].astype(F32) for i in range(NB)]
    x = spectrum(blocks, tw_ref, mh_ref, ml_ref, buf)
    xr, xi, hr, hi = x[:, :G], x[:, G:], spec_ref[:, :G], spec_ref[:, G:]
    buf[:, :G] = xr * hr - xi * hi
    buf[:, G:] = xr * hi + xi * hr
    buf[...] = dot3(buf[...], nh_ref[...], nl_ref[...])
    z = []
    for p in range(NB):
        re, im = buf[p * CH : (p + 1) * CH, :G], buf[p * CH : (p + 1) * CH, G:]
        c, s = tw_ref[0, p : p + 1, :], tw_ref[1, p : p + 1, :]
        z.append((re * c - im * s, im * c + re * s))
    z = fft(z, 1.0)
    skip = skip_ref[...]
    lane = lax.broadcasted_iota(jnp.int32, (CH, G), 1)
    for i, (re, im) in enumerate(z):
        ang = 2.0 * math.pi * DELTA * i / NB
        y = (re * math.cos(ang) - im * math.sin(ang)) * (1.0 / SEQ)
        y = in_ref[i, CH : 2 * CH, :].astype(F32) * (y + skip * in_ref[i, 0:CH, :].astype(F32))
        y = jnp.where(lane + i * G < valid, y, 0.0).astype(BF)
        for k in range(4):
            out_ref[k, i] = y


def weights_kernel(idx_ref, q_ref, own_ref, other_ref, w_ref, total_ref, keys, scores):
    k, core, valid = idx_ref[3], idx_ref[4], idx_ref[2]
    flip = core == 1
    for s in range(NB):
        own, other = own_ref[s], other_ref[s]
        keys[s * G : s * G + 64] = jnp.where(flip, other, own)
        keys[s * G + 64 : (s + 1) * G] = jnp.where(flip, own, other)
    factor = math.log2(math.e) / math.sqrt(HD)
    row = lax.broadcasted_iota(jnp.int32, (2 * G, G), 0)
    lane = lax.broadcasted_iota(jnp.int32, (2 * G, G), 1)
    for t in range(4):
        q = q_ref[2 * t : 2 * t + 2].reshape(2 * G, HD)
        limit = jnp.minimum(row + (8 * t + 2 * k) * G, valid - 1)
        top = None
        for m in range(4 * t + 4):
            s = lax.dot_general(
                q, keys[m * 2 * G : (m + 1) * 2 * G], NT, preferred_element_type=F32
            )
            for u in range(2):
                n = 2 * m + u
                part = s[:, u * G : (u + 1) * G]
                if n >= 8 * t:
                    part = jnp.where(lane + n * G <= limit, part, -1e30)
                scores[:, n * G : (n + 1) * G] = part
                top = part if top is None else jnp.maximum(top, part)
        top = jnp.max(top, axis=1, keepdims=True)
        total = None
        for n in range(8 * t + 8):
            part = jnp.exp2((scores[:, n * G : (n + 1) * G] - top) * factor)
            w_ref[2 * t * G : (2 * t + 2) * G, n * G : (n + 1) * G] = part.astype(BF)
            total = part if total is None else total + part
        total = jnp.sum(total, axis=1, keepdims=True)
        total_ref[2 * t * G : (2 * t + 2) * G, :] = jnp.broadcast_to(total, (2 * G, G))


def values_kernel(idx_ref, w_ref, total_ref, v_ref, msg_ref, sum_ref, vals):
    k, core = idx_ref[3], idx_ref[4]
    for s in range(NB):
        block = v_ref[:, s].reshape(64, G)
        vals[0:64, s * G : (s + 1) * G] = block
        vals[64:128, s * G : (s + 1) * G] = block
    lane = lax.broadcasted_iota(jnp.int32, (64, G), 1)
    mine = (lane < 64) != (core == 1)
    ones = jnp.where(lax.broadcasted_iota(jnp.int32, (8, G), 1) < 64, 1.0, 0.0).astype(BF)
    for t in range(4):
        n = (8 * t + 8) * G
        rows = slice(2 * t * G, (2 * t + 2) * G)
        out = lax.dot_general(w_ref[rows, 0:n], vals[:, 0:n], NT, preferred_element_type=F32)
        out = out / total_ref[rows, :]
        high, low = split(out * out)
        sums = lax.dot_general(ones, high, NT, preferred_element_type=F32) + lax.dot_general(
            ones, low, NT, preferred_element_type=F32
        )
        for c in range(2):
            j = 2 * t + c
            a = out[c * G : c * G + 64]
            b = out[c * G + 64 : (c + 1) * G]
            msg_ref[j, 0:64, :] = jnp.where(mine, a, b).astype(BF)
            msg_ref[j, 64:128, :] = v_ref[:, 8 * t + 2 * k + c].reshape(64, G)
            sum_ref[8 * j : 8 * j + 8, :] = sums[:, c * G : (c + 1) * G]


def final_kernel(idx_ref, msg_ref, sum_ref, hyena_ref, attn_ref):
    valid, own = idx_ref[2], idx_ref[5]
    total = jnp.sum(sum_ref[...], axis=0, keepdims=True)
    norm = jnp.sqrt(total * (1.0 / DW) + 1e-06)
    inv = jnp.broadcast_to(1.0 / norm, (G, G)).T
    row = lax.broadcasted_iota(jnp.int32, (G, G), 0)
    inv = jnp.where(row + own * G < valid, inv, 0.0)
    left = lax.broadcasted_iota(jnp.int32, (64, G), 1) < 64
    for h in range(4):
        cols = slice(h * HD, (h + 1) * HD)
        p0 = msg_ref[2 * h, 0:64, :].astype(F32)
        p1 = msg_ref[2 * h + 1, 0:64, :].astype(F32)
        low = jnp.where(left, p0, p1)
        high = pltpu.roll(jnp.where(left, p1, p0), 64, 1)
        attn_ref[0:64, cols] = (low * inv[0:64]).astype(BF)
        attn_ref[64:128, cols] = (high * inv[64:128]).astype(BF)
        hy = msg_ref[2 * h : 2 * h + 2, 64:128, :].reshape(G, G).astype(F32)
        hyena_ref[:, cols] = hy.T.astype(BF)


def sds(shape, dtype):
    return jax.ShapeDtypeStruct(shape, dtype)


def full(*shape):
    return pl.BlockSpec(shape, lambda *_: (0,) * len(shape))


def call(kernel, out_shape, in_specs, scratch=(), cost=(1e7, 1 << 20), vmem=24):
    outs = out_shape if isinstance(out_shape, (tuple, list)) else (out_shape,)
    specs = [full(*o.shape) for o in outs]
    return pl.pallas_call(
        kernel,
        out_shape=out_shape,
        grid_spec=pltpu.PrefetchScalarGridSpec(
            num_scalar_prefetch=1,
            grid=(1,),
            in_specs=in_specs,
            out_specs=specs if isinstance(out_shape, (tuple, list)) else specs[0],
            scratch_shapes=list(scratch),
        ),
        compiler_params=pltpu.CompilerParams(vmem_limit_bytes=vmem << 20),
        cost_estimate=pl.CostEstimate(
            flops=int(cost[0]), bytes_accessed=int(cost[1]), transcendentals=0
        ),
    )


def shards(
    hyena_gate, hyena_key, hyena_value, filter_taps, skip_weight, queries, attn_keys, valid_length
):
    own = lax.axis_index("ctx").astype(jnp.int32)
    h, k, core = own // 8, (own // 2) % 4, own % 2
    first = core * 64 + k * CH
    idx = jnp.stack([h, first, valid_length[0], k, core, own])
    high, low, high_t, low_t, twiddle = (jnp.asarray(t) for t in tables())
    skip = lax.dynamic_slice_in_dim(skip_weight, h * HD + first, CH, 0)
    skip = jnp.broadcast_to(skip[:, None], (CH, G))
    a2a = functools.partial(lax.all_to_all, split_axis=0, concat_axis=0, tiled=True)

    block = full(G, 4 * HD)
    msg, qmsg = pl.pallas_call(
        pre_kernel,
        out_shape=(sds((NB, 96, G), BF), sds((8, G, HD), BF)),
        compiler_params=pltpu.CompilerParams(vmem_limit_bytes=16 << 20),
        cost_estimate=pl.CostEstimate(flops=1000000, bytes_accessed=2 << 20, transcendentals=0),
    )(hyena_key, hyena_value, hyena_gate, attn_keys, queries)
    got = a2a(msg, "ctx")
    got_q = a2a(qmsg, "ctx", axis_index_groups=COLS)

    spec = call(
        taps_kernel,
        sds((NB * CH, 2 * G), F32),
        [
            pl.BlockSpec((SEQ, G), lambda i, idx: (0, idx[0])),
            full(2, NB, G),
            full(2 * G, 2 * G),
            full(2 * G, 2 * G),
        ],
        [pltpu.VMEM((NB * CH, 2 * G), F32)],
        cost=(2e9, 4 << 20),
    )(idx, filter_taps, twiddle, high, low)

    got_other = lax.ppermute(got, "ctx", CORES)
    values = call(
        conv_kernel,
        sds((4, NB, CH, G), BF),
        [
            pl.BlockSpec((NB, 2 * CH, G), lambda i, idx: (0, 2, 0)),
            full(NB * CH, 2 * G),
            full(CH, G),
            full(2, NB, G),
            full(2 * G, 2 * G),
            full(2 * G, 2 * G),
            full(2 * G, 2 * G),
            full(2 * G, 2 * G),
        ],
        [pltpu.VMEM((NB * CH, 2 * G), F32)],
        cost=(2e9, 4 << 20),
    )(idx, got, spec, skip, twiddle, high, low, high_t, low_t)
    got_v = a2a(values, "ctx", axis_index_groups=ROWS)

    weights, totals = call(
        weights_kernel,
        (sds((8 * G, SEQ), BF), sds((8 * G, G), F32)),
        [
            full(8, G, HD),
            pl.BlockSpec((NB, 64, G), lambda i, idx: (0, 0, 0)),
            pl.BlockSpec((NB, 64, G), lambda i, idx: (0, 0, 0)),
        ],
        [pltpu.VMEM((SEQ, HD), BF), pltpu.VMEM((2 * G, SEQ), F32)],
        cost=(4e9, 16 << 20),
    )(idx, got_q, got, got_other)

    back, sums = call(
        values_kernel,
        (sds((8, G, G), BF), sds((64, G), F32)),
        [full(8 * G, SEQ), full(8 * G, G), full(4, NB, CH, G)],
        [pltpu.VMEM((G, SEQ), BF)],
        cost=(2e9, 8 << 20),
        vmem=32,
    )(idx, weights, totals, got_v)
    got_back = a2a(back, "ctx", axis_index_groups=COLS)
    got_sums = a2a(sums, ("ctx", "tp"), axis_index_groups=COLS_TP)

    return call(
        final_kernel,
        (sds((G, 4 * HD), BF), sds((G, 4 * HD), BF)),
        [full(8, G, G), full(64, G)],
        cost=(1e6, 1 << 20),
    )(idx, got_back, got_sums)


def solution(mesh):
    in_specs = (
        P("ctx", "tp"),
        P("ctx", "tp"),
        P("ctx", "tp"),
        P(None, "tp"),
        P("tp"),
        P("ctx", "tp"),
        P("ctx", "tp"),
        P(),
    )
    out_specs = (P("ctx", "tp"), P("ctx", "tp"))
    return jax.shard_map(shards, mesh=mesh, in_specs=in_specs, out_specs=out_specs, check_vma=False)
```

```python
import math

import jax
import jax.numpy as jnp
import numpy as np
from jax import lax
from jax.experimental import pallas as pl
from jax.experimental.pallas import tpu as pltpu
from jax.sharding import PartitionSpec as P


HD = 128
DW = 4096
SEQ = 4096
G = 128
NB = SEQ // G
CH = 16
DELTA = 0.25

COLS = [[8 * y + 2 * x + e for y in range(4) for e in range(2)] for x in range(4)]
CORES = [(i, i ^ 1) for i in range(32)]


def along_y(d):
    return [(i, (i + 8 * d) % 32) for i in range(32)]


def along_x(d):
    return [(i, 8 * (i // 8) + (i + 2 * d) % 8) for i in range(32)]


BF = jnp.bfloat16
F32 = jnp.float32
NT = (((1,), (1,)), ((), ()))


def tables():
    b = np.arange(G)
    ang = 2.0 * np.pi * np.outer(b, b) / G
    c, s = np.cos(ang), np.sin(ang)
    fwd = np.block([[c, -s], [s, c]]).astype(np.float32)
    high = fwd.astype(jnp.bfloat16)
    low = (fwd - high.astype(np.float32)).astype(jnp.bfloat16)
    phase = 2.0 * np.pi * np.outer(np.arange(NB) + DELTA, b) / SEQ
    twiddle = np.stack([np.cos(phase), np.sin(phase)]).astype(np.float32)
    return high, low, high.T.copy(), low.T.copy(), twiddle


def cmul_const(z, ang):
    re, im = z
    c, s = math.cos(ang), math.sin(ang)
    if im is None:
        return (re * c, re * s) if abs(s) > 1e-12 else (re, jnp.zeros_like(re))
    if abs(s) < 1e-12:
        return (re, im) if c > 0 else (-re, -im)
    if abs(c) < 1e-12:
        return (-im, re) if s > 0 else (im, -re)
    return (re * c - im * s, re * s + im * c)


def fft(z, sign):
    n = len(z)
    if n == 1:
        return z
    half = n // 2
    up, down = [], []
    for j in range(half):
        (ar, ai), (br, bi) = z[j], z[j + half]
        up.append((ar + br, ai + bi))
        down.append(cmul_const((ar - br, ai - bi), sign * 2.0 * math.pi * j / n))
    even, odd = fft(up, sign), fft(down, sign)
    out = []
    for e, o in zip(even, odd):
        out += [e, o]
    return out


def split(x):
    high = x.astype(BF)
    return high, (x - high.astype(F32)).astype(BF)


def dot3(x, m_high, m_low):
    high, low = split(x)
    return (
        jnp.dot(high, m_high, preferred_element_type=F32)
        + jnp.dot(low, m_high, preferred_element_type=F32)
        + jnp.dot(high, m_low, preferred_element_type=F32)
    )


def spectrum(blocks, tw_ref, mh_ref, ml_ref, buf):
    z = [cmul_const((x, None), -2.0 * math.pi * DELTA * i / NB) for i, x in enumerate(blocks)]
    z = fft(z, -1.0)
    for p, (re, im) in enumerate(z):
        c, s = tw_ref[0, p : p + 1, :], tw_ref[1, p : p + 1, :]
        buf[p * CH : (p + 1) * CH, :G] = re * c + im * s
        buf[p * CH : (p + 1) * CH, G:] = im * c - re * s
    return dot3(buf[...], mh_ref[...], ml_ref[...])


def load(pairs, sems):
    copies = [pltpu.make_async_copy(a, b, sems.at[n]) for n, (a, b) in enumerate(pairs)]
    for copy in copies:
        copy.start()
    return copies


def pre_kernel(idx_ref, key_hbm, value_hbm, gate_hbm, attn_hbm, query_hbm, *refs):
    msg_ref, q_refs, (key_ref, value_ref, gate_ref, attn_ref, query_ref, sems) = (
        refs[0],
        refs[1:5],
        refs[5:],
    )
    copies = load(
        [
            (key_hbm, key_ref),
            (value_hbm, value_ref),
            (gate_hbm, gate_ref),
            (attn_hbm, attn_ref),
            (query_hbm, query_ref),
        ],
        sems,
    )
    copies[0].wait()
    copies[1].wait()
    for h in range(4):
        cols = slice(h * HD, (h + 1) * HD)
        mixed = (key_ref[:, cols].astype(F32) * value_ref[:, cols].astype(F32)).T.astype(BF)
        for c in range(2):
            for k in range(4):
                rows = slice(c * 64 + k * CH, c * 64 + (k + 1) * CH)
                msg_ref[8 * h + 2 * k + c, 64:80, :] = mixed[rows]
    copies[2].wait()
    for h in range(4):
        gate = gate_ref[:, h * HD : (h + 1) * HD].astype(F32).T.astype(BF)
        for c in range(2):
            for k in range(4):
                rows = slice(c * 64 + k * CH, c * 64 + (k + 1) * CH)
                msg_ref[8 * h + 2 * k + c, 80:96, :] = gate[rows]
    copies[3].wait()
    for h in range(4):
        for c in range(2):
            for k in range(4):
                msg_ref[8 * h + 2 * k + c, 0:64, :] = attn_ref[
                    c * 64 : (c + 1) * 64, h * HD : (h + 1) * HD
                ]
    copies[4].wait()
    for d in range(4):
        col = pl.multiple_of(lax.rem(idx_ref[0] + d, 4) * HD, HD)
        q_refs[d][...] = query_ref[:, pl.ds(col, HD)]


def taps_kernel(idx_ref, taps_hbm, tw_hbm, mh_hbm, ml_hbm, *refs):
    out_ref, taps_ref, buf, tw_ref, mh_ref, ml_ref, sems = refs[-7:]
    col = pl.multiple_of(idx_ref[0] * HD, HD)
    parts = 4
    size = SEQ // parts
    copies = load(
        [
            (
                taps_hbm.at[pl.ds(n * size, size), pl.ds(col, HD)],
                taps_ref.at[pl.ds(n * size, size), :],
            )
            for n in range(parts)
        ]
        + [(tw_hbm, tw_ref), (mh_hbm, mh_ref), (ml_hbm, ml_ref)],
        sems,
    )
    first = idx_ref[1]
    row = lax.broadcasted_iota(jnp.int32, (CH, G), 0)
    lane = lax.broadcasted_iota(jnp.int32, (CH, G), 1)
    pick = jnp.where(lane == row + first, 1.0, 0.0).astype(BF)
    for copy in copies:
        copy.wait()
    blocks = [
        lax.dot_general(pick, taps_ref[i * G : (i + 1) * G, :], NT, preferred_element_type=F32)
        for i in range(NB)
    ]
    out_ref[...] = spectrum(blocks, tw_ref, mh_ref, ml_ref, buf)


def conv_kernel(
    idx_ref, in_ref, spec_ref, skip_ref, tw_ref, mh_ref, ml_ref, nh_ref, nl_ref, out_ref, buf
):
    valid = idx_ref[2]
    blocks = [in_ref[i, 64:80, :].astype(F32) for i in range(NB)]
    x = spectrum(blocks, tw_ref, mh_ref, ml_ref, buf)
    xr, xi, hr, hi = x[:, :G], x[:, G:], spec_ref[:, :G], spec_ref[:, G:]
    buf[:, :G] = xr * hr - xi * hi
    buf[:, G:] = xr * hi + xi * hr
    buf[...] = dot3(buf[...], nh_ref[...], nl_ref[...])
    z = []
    for p in range(NB):
        re, im = buf[p * CH : (p + 1) * CH, :G], buf[p * CH : (p + 1) * CH, G:]
        c, s = tw_ref[0, p : p + 1, :], tw_ref[1, p : p + 1, :]
        z.append((re * c - im * s, im * c + re * s))
    z = fft(z, 1.0)
    row = lax.broadcasted_iota(jnp.int32, (CH, G), 0)
    lane = lax.broadcasted_iota(jnp.int32, (CH, G), 1)
    skip = jnp.zeros((CH, G), F32)
    for r in range(CH):
        skip = jnp.where(row == r, skip_ref[idx_ref[0] * HD + idx_ref[1] + r], skip)
    for i, (re, im) in enumerate(z):
        ang = 2.0 * math.pi * DELTA * i / NB
        y = (re * math.cos(ang) - im * math.sin(ang)) * (1.0 / SEQ)
        y = in_ref[i, 80:96, :].astype(F32) * (y + skip * in_ref[i, 64:80, :].astype(F32))
        out_ref[i] = jnp.where(lane + i * G < valid, y, 0.0).astype(BF)


def weights_kernel(idx_ref, *refs):
    q_refs, own_ref, other_ref, w_ref, total_ref = refs[:8], refs[8], refs[9], refs[10], refs[11]
    qs, keys, scores = refs[12:]
    head, k, core, valid = idx_ref[0], idx_ref[3], idx_ref[4], idx_ref[2]
    flip = core == 1
    for d in range(4):
        own, other = q_refs[d][...], q_refs[4 + d][...]
        qs[d, 0:G] = jnp.where(flip, other, own)
        qs[d, G : 2 * G] = jnp.where(flip, own, other)
    for s in range(NB):
        own, other = own_ref[s, 0:64], other_ref[s, 0:64]
        keys[s * G : s * G + 64] = jnp.where(flip, other, own)
        keys[s * G + 64 : (s + 1) * G] = jnp.where(flip, own, other)
    factor = math.log2(math.e) / math.sqrt(HD)
    row = lax.broadcasted_iota(jnp.int32, (2 * G, G), 0)
    lane = lax.broadcasted_iota(jnp.int32, (2 * G, G), 1)
    for t in range(4):
        q = qs[lax.rem(head + 4 - t, 4)]
        limit = jnp.minimum(row + (8 * t + 2 * k) * G, valid - 1)
        top = None
        for m in range(4 * t + 4):
            s = lax.dot_general(
                q, keys[m * 2 * G : (m + 1) * 2 * G], NT, preferred_element_type=F32
            )
            for u in range(2):
                n = 2 * m + u
                part = s[:, u * G : (u + 1) * G]
                if n >= 8 * t:
                    part = jnp.where(lane + n * G <= limit, part, -1e30)
                scores[:, n * G : (n + 1) * G] = part
                top = part if top is None else jnp.maximum(top, part)
        top = jnp.max(top, axis=1, keepdims=True)
        total = None
        for n in range(8 * t + 8):
            part = jnp.exp2((scores[:, n * G : (n + 1) * G] - top) * factor)
            w_ref[2 * t * G : (2 * t + 2) * G, n * G : (n + 1) * G] = part.astype(BF)
            total = part if total is None else total + part
        total = jnp.sum(total, axis=1, keepdims=True)
        total_ref[2 * t * G : (2 * t + 2) * G, :] = jnp.broadcast_to(total, (2 * G, G))


def values_kernel(idx_ref, w_ref, total_ref, v0, v1, v2, v3, msg_ref, vals):
    k, core = idx_ref[3], idx_ref[4]
    for d, v_ref in enumerate((v0, v1, v2, v3)):
        row = pl.multiple_of(lax.rem(k + 4 - d, 4) * CH, CH)
        for s in range(NB):
            block = v_ref[s]
            vals[pl.ds(row, CH), s * G : (s + 1) * G] = block
            vals[pl.ds(row + 64, CH), s * G : (s + 1) * G] = block
    lane = lax.broadcasted_iota(jnp.int32, (64, G), 1)
    mine = (lane < 64) != (core == 1)
    for t in range(4):
        n = (8 * t + 8) * G
        rows = slice(2 * t * G, (2 * t + 2) * G)
        out = lax.dot_general(w_ref[rows, 0:n], vals[:, 0:n], NT, preferred_element_type=F32)
        out = out / total_ref[rows, :]
        for c in range(2):
            j = 2 * t + c
            a = out[c * G : c * G + 64]
            b = out[c * G + 64 : (c + 1) * G]
            msg_ref[j, 0:64, :] = jnp.where(mine, a, b).astype(BF)
            col = pl.multiple_of((8 * t + 2 * k + c) * G, G)
            msg_ref[j, 64:128, :] = vals[0:64, pl.ds(col, G)]


def gather_kernel(msg_ref, attended_ref, sum_ref):
    left = lax.broadcasted_iota(jnp.int32, (64, G), 1) < 64
    ones = jnp.ones((8, G), BF)
    sums = jnp.zeros((8, G), F32)
    for h in range(4):
        cols = slice(h * HD, (h + 1) * HD)
        p0 = msg_ref[2 * h, 0:64, :].astype(F32)
        p1 = msg_ref[2 * h + 1, 0:64, :].astype(F32)
        low = jnp.where(left, p0, p1)
        high = pltpu.roll(jnp.where(left, p1, p0), 64, 1)
        both = jnp.concatenate([low, high], axis=0)
        attended_ref[:, cols] = both.astype(BF)
        for part in split(both * both):
            sums += lax.dot_general(ones, part, NT, preferred_element_type=F32)
    sum_ref[...] = sums


def hyena_kernel(msg_ref, hyena_ref):
    for h in range(4):
        block = msg_ref[2 * h : 2 * h + 2, 64:128, :].reshape(G, G).astype(F32)
        hyena_ref[:, h * HD : (h + 1) * HD] = block.T.astype(BF)


def final_kernel(idx_ref, attended_ref, sum_ref, attn_ref):
    valid, own = idx_ref[2], idx_ref[5]
    total = jnp.sum(sum_ref[...], axis=0, keepdims=True)
    norm = jnp.sqrt(total * (1.0 / DW) + 1e-06)
    inv = jnp.broadcast_to(1.0 / norm, (G, G)).T
    row = lax.broadcasted_iota(jnp.int32, (G, G), 0)
    inv = jnp.where(row + own * G < valid, inv, 0.0)
    for h in range(4):
        cols = slice(h * HD, (h + 1) * HD)
        attn_ref[:, cols] = (attended_ref[:, cols].astype(F32) * inv).astype(BF)


def sds(shape, dtype):
    return jax.ShapeDtypeStruct(shape, dtype)


VM = pl.BlockSpec(memory_space=pltpu.MemorySpace.VMEM)
SM = pl.BlockSpec(memory_space=pltpu.MemorySpace.SMEM)
AN = pl.BlockSpec(memory_space=pl.ANY)
HB = pl.BlockSpec(memory_space=pltpu.MemorySpace.HBM)


def call(kernel, out_shape, in_specs, scratch=(), out_specs=None, us=1, vmem=16):
    many = isinstance(out_shape, (tuple, list))
    return pl.pallas_call(
        kernel,
        out_shape=out_shape,
        in_specs=in_specs,
        out_specs=out_specs or ([VM] * len(out_shape) if many else VM),
        scratch_shapes=list(scratch),
        compiler_params=pltpu.CompilerParams(vmem_limit_bytes=vmem << 20),
        cost_estimate=pl.CostEstimate(
            flops=int(us * 10**9), bytes_accessed=int(us * 2 * 10**6), transcendentals=0
        ),
    )


def dma(n):
    return pltpu.SemaphoreType.DMA((n,))


def shards(
    hyena_gate, hyena_key, hyena_value, filter_taps, skip_weight, queries, attn_keys, valid_length
):
    own = lax.axis_index("ctx").astype(jnp.int32)
    head = lax.shift_right_logical(own, 3)
    k = lax.bitwise_and(lax.shift_right_logical(own, 1), 3)
    core = lax.bitwise_and(own, 1)
    idx = jnp.stack([head, core * 64 + k * CH, valid_length[0], k, core, own])
    high, low, high_t, low_t, twiddle = (jnp.asarray(t) for t in tables())

    block = pltpu.VMEM((G, 4 * HD), BF)
    msg, *q = call(
        pre_kernel,
        (sds((NB, 96, G), BF),) + (sds((G, HD), BF),) * 4,
        [SM] + [HB] * 5,
        [block] * 5 + [dma(5)],
        vmem=60,
    )(idx, hyena_key, hyena_value, hyena_gate, attn_keys, queries)
    got = lax.all_to_all(msg, "ctx", 0, 0, tiled=True)
    q = [q[0]] + [lax.ppermute(q[d], "ctx", along_y(d)) for d in (1, 2, 3)]
    q += [lax.ppermute(x, "ctx", CORES) for x in q]
    spec = call(
        taps_kernel,
        sds((NB * CH, 2 * G), F32),
        [SM, HB] + [AN] * 10,
        [
            pltpu.VMEM((SEQ, HD), BF),
            pltpu.VMEM((NB * CH, 2 * G), F32),
            pltpu.VMEM((2, NB, G), F32),
            pltpu.VMEM((2 * G, 2 * G), BF),
            pltpu.VMEM((2 * G, 2 * G), BF),
            dma(7),
        ],
        us=2,
        vmem=50,
    )(idx, filter_taps, twiddle, high, low, *q[1:])
    got_other = lax.ppermute(got, "ctx", CORES)
    values = call(
        conv_kernel,
        sds((NB, CH, G), BF),
        [SM, VM, VM, SM] + [VM] * 5,
        [pltpu.VMEM((NB * CH, 2 * G), F32)],
        us=3,
    )(idx, got, spec, skip_weight, twiddle, high, low, high_t, low_t)
    v = [values] + [lax.ppermute(values, "ctx", along_x(d)) for d in (1, 2, 3)]
    weights, totals = call(
        weights_kernel,
        (sds((8 * G, SEQ), BF), sds((8 * G, G), F32)),
        [SM] + [VM] * 8 + [VM] * 2,
        [pltpu.VMEM((4, 2 * G, HD), BF), pltpu.VMEM((SEQ, HD), BF), pltpu.VMEM((2 * G, SEQ), F32)],
        us=4,
    )(idx, *q, got, got_other)
    back = call(
        values_kernel,
        sds((8, G, G), BF),
        [SM] + [VM] * 6,
        [pltpu.VMEM((G, SEQ), BF)],
        us=4,
    )(idx, weights, totals, *v)
    got_back = lax.all_to_all(back, "ctx", 0, 0, tiled=True, axis_index_groups=COLS)
    attended, sums = call(gather_kernel, (sds((G, 4 * HD), BF), sds((8, G), F32)), [VM])(got_back)
    sums = lax.all_to_all(sums, "tp", 0, 0, tiled=True)
    hyena_out = call(hyena_kernel, sds((G, 4 * HD), BF), [VM])(got_back)
    attn_out = call(final_kernel, sds((G, 4 * HD), BF), [SM, VM, VM])(idx, attended, sums)
    return hyena_out, attn_out


def solution(mesh):
    in_specs = (
        P("ctx", "tp"),
        P("ctx", "tp"),
        P("ctx", "tp"),
        P(None, "tp"),
        P("tp"),
        P("ctx", "tp"),
        P("ctx", "tp"),
        P(),
    )
    out_specs = (P("ctx", "tp"), P("ctx", "tp"))
    return jax.shard_map(shards, mesh=mesh, in_specs=in_specs, out_specs=out_specs, check_vma=False)
```

```python
import math

import jax
import jax.numpy as jnp
import numpy as np
from jax import lax
from jax.experimental import pallas as pl
from jax.experimental.pallas import tpu as pltpu
from jax.sharding import PartitionSpec as P


HD = 128
DW = 4096
SEQ = 4096
G = 128
NB = SEQ // G
CH = 16
DELTA = 0.25

COLS = [[8 * y + 2 * x + e for y in range(4) for e in range(2)] for x in range(4)]
CORES = [(i, i ^ 1) for i in range(32)]


def along_y(d):
    return [(i, (i + 8 * d) % 32) for i in range(32)]


def along_x(d):
    return [(i, 8 * (i // 8) + (i + 2 * d) % 8) for i in range(32)]


BF = jnp.bfloat16
F32 = jnp.float32
NT = (((1,), (1,)), ((), ()))


def tables():
    b = np.arange(G)
    ang = 2.0 * np.pi * np.outer(b, b) / G
    c, s = np.cos(ang), np.sin(ang)
    fwd = np.block([[c, -s], [s, c]]).astype(np.float32)
    high = fwd.astype(jnp.bfloat16)
    low = (fwd - high.astype(np.float32)).astype(jnp.bfloat16)
    phase = 2.0 * np.pi * np.outer(np.arange(NB) + DELTA, b) / SEQ
    twiddle = np.stack([np.cos(phase), np.sin(phase)]).astype(np.float32)
    return high, low, high.T.copy(), low.T.copy(), twiddle


def cmul_const(z, ang):
    re, im = z
    c, s = math.cos(ang), math.sin(ang)
    if im is None:
        return (re * c, re * s) if abs(s) > 1e-12 else (re, jnp.zeros_like(re))
    if abs(s) < 1e-12:
        return (re, im) if c > 0 else (-re, -im)
    if abs(c) < 1e-12:
        return (-im, re) if s > 0 else (im, -re)
    return (re * c - im * s, re * s + im * c)


def fft(z, sign):
    n = len(z)
    if n == 1:
        return z
    half = n // 2
    up, down = [], []
    for j in range(half):
        (ar, ai), (br, bi) = z[j], z[j + half]
        up.append((ar + br, ai + bi))
        down.append(cmul_const((ar - br, ai - bi), sign * 2.0 * math.pi * j / n))
    even, odd = fft(up, sign), fft(down, sign)
    out = []
    for e, o in zip(even, odd):
        out += [e, o]
    return out


def split(x):
    high = x.astype(BF)
    return high, (x - high.astype(F32)).astype(BF)


def dot3(x, m_high, m_low):
    high, low = split(x)
    return (
        jnp.dot(high, m_high, preferred_element_type=F32)
        + jnp.dot(low, m_high, preferred_element_type=F32)
        + jnp.dot(high, m_low, preferred_element_type=F32)
    )


def spectrum(blocks, tw_ref, mh_ref, ml_ref, buf):
    z = [cmul_const((x, None), -2.0 * math.pi * DELTA * i / NB) for i, x in enumerate(blocks)]
    z = fft(z, -1.0)
    for p, (re, im) in enumerate(z):
        c, s = tw_ref[0, p : p + 1, :], tw_ref[1, p : p + 1, :]
        buf[p * CH : (p + 1) * CH, :G] = re * c + im * s
        buf[p * CH : (p + 1) * CH, G:] = im * c - re * s
    return dot3(buf[...], mh_ref[...], ml_ref[...])


def place():
    own = lax.axis_index("ctx").astype(jnp.int32)
    k = lax.bitwise_and(lax.shift_right_logical(own, 1), 3)
    return own, lax.shift_right_logical(own, 3), k, lax.bitwise_and(own, 1)


def load(pairs, sems):
    copies = [pltpu.make_async_copy(a, b, sems.at[n]) for n, (a, b) in enumerate(pairs)]
    for copy in copies:
        copy.start()
    return copies


def pre_kernel(key_hbm, value_hbm, gate_hbm, attn_hbm, query_hbm, *refs):
    msg_ref, q_refs, (key_ref, value_ref, gate_ref, attn_ref, query_ref, sems) = (
        refs[0],
        refs[1:5],
        refs[5:],
    )
    copies = load(
        [
            (key_hbm, key_ref),
            (value_hbm, value_ref),
            (gate_hbm, gate_ref),
            (attn_hbm, attn_ref),
            (query_hbm, query_ref),
        ],
        sems,
    )
    copies[0].wait()
    copies[1].wait()
    for h in range(4):
        cols = slice(h * HD, (h + 1) * HD)
        mixed = (key_ref[:, cols].astype(F32) * value_ref[:, cols].astype(F32)).T.astype(BF)
        for c in range(2):
            for k in range(4):
                rows = slice(c * 64 + k * CH, c * 64 + (k + 1) * CH)
                msg_ref[8 * h + 2 * k + c, 64:80, :] = mixed[rows]
    copies[2].wait()
    for h in range(4):
        gate = gate_ref[:, h * HD : (h + 1) * HD].astype(F32).T.astype(BF)
        for c in range(2):
            for k in range(4):
                rows = slice(c * 64 + k * CH, c * 64 + (k + 1) * CH)
                msg_ref[8 * h + 2 * k + c, 80:96, :] = gate[rows]
    copies[3].wait()
    for h in range(4):
        for c in range(2):
            for k in range(4):
                msg_ref[8 * h + 2 * k + c, 0:64, :] = attn_ref[
                    c * 64 : (c + 1) * 64, h * HD : (h + 1) * HD
                ]
    copies[4].wait()
    head = place()[1]
    for d in range(4):
        col = pl.multiple_of(lax.rem(head + d, 4) * HD, HD)
        q_refs[d][...] = query_ref[:, pl.ds(col, HD)]


def taps_kernel(
    taps_hbm, tw_hbm, mh_hbm, ml_hbm, out_ref, taps_ref, buf, tw_ref, mh_ref, ml_ref, sems
):
    _, head, k, core = place()
    col = pl.multiple_of(head * HD, HD)
    parts = 4
    size = SEQ // parts
    copies = load(
        [
            (
                taps_hbm.at[pl.ds(n * size, size), pl.ds(col, HD)],
                taps_ref.at[pl.ds(n * size, size), :],
            )
            for n in range(parts)
        ]
        + [(tw_hbm, tw_ref), (mh_hbm, mh_ref), (ml_hbm, ml_ref)],
        sems,
    )
    first = core * 64 + k * CH
    row = lax.broadcasted_iota(jnp.int32, (CH, G), 0)
    lane = lax.broadcasted_iota(jnp.int32, (CH, G), 1)
    pick = jnp.where(lane == row + first, 1.0, 0.0).astype(BF)
    for copy in copies:
        copy.wait()
    blocks = [
        lax.dot_general(pick, taps_ref[i * G : (i + 1) * G, :], NT, preferred_element_type=F32)
        for i in range(NB)
    ]
    out_ref[...] = spectrum(blocks, tw_ref, mh_ref, ml_ref, buf)


def conv_kernel(
    valid_ref, in_ref, spec_ref, skip_ref, tw_ref, mh_ref, ml_ref, nh_ref, nl_ref, out_ref, buf
):
    valid = valid_ref[0]
    _, head, k, core = place()
    blocks = [in_ref[i, 64:80, :].astype(F32) for i in range(NB)]
    x = spectrum(blocks, tw_ref, mh_ref, ml_ref, buf)
    xr, xi, hr, hi = x[:, :G], x[:, G:], spec_ref[:, :G], spec_ref[:, G:]
    buf[:, :G] = xr * hr - xi * hi
    buf[:, G:] = xr * hi + xi * hr
    buf[...] = dot3(buf[...], nh_ref[...], nl_ref[...])
    z = []
    for p in range(NB):
        re, im = buf[p * CH : (p + 1) * CH, :G], buf[p * CH : (p + 1) * CH, G:]
        c, s = tw_ref[0, p : p + 1, :], tw_ref[1, p : p + 1, :]
        z.append((re * c - im * s, im * c + re * s))
    z = fft(z, 1.0)
    row = lax.broadcasted_iota(jnp.int32, (CH, G), 0)
    lane = lax.broadcasted_iota(jnp.int32, (CH, G), 1)
    skip = jnp.zeros((CH, G), F32)
    for r in range(CH):
        skip = jnp.where(row == r, skip_ref[head * HD + core * 64 + k * CH + r], skip)
    for i, (re, im) in enumerate(z):
        ang = 2.0 * math.pi * DELTA * i / NB
        y = (re * math.cos(ang) - im * math.sin(ang)) * (1.0 / SEQ)
        y = in_ref[i, 80:96, :].astype(F32) * (y + skip * in_ref[i, 64:80, :].astype(F32))
        out_ref[i] = jnp.where(lane + i * G < valid, y, 0.0).astype(BF)


def weights_kernel(valid_ref, *refs):
    q_refs, own_ref, other_ref, w_ref, total_ref = refs[:8], refs[8], refs[9], refs[10], refs[11]
    qs, keys, scores = refs[12:]
    _, head, k, core = place()
    valid = valid_ref[0]
    flip = core == 1
    for d in range(4):
        own, other = q_refs[d][...], q_refs[4 + d][...]
        qs[d, 0:G] = jnp.where(flip, other, own)
        qs[d, G : 2 * G] = jnp.where(flip, own, other)
    for s in range(NB):
        own, other = own_ref[s, 0:64], other_ref[s, 0:64]
        keys[s * G : s * G + 64] = jnp.where(flip, other, own)
        keys[s * G + 64 : (s + 1) * G] = jnp.where(flip, own, other)
    factor = math.log2(math.e) / math.sqrt(HD)
    row = lax.broadcasted_iota(jnp.int32, (2 * G, G), 0)
    lane = lax.broadcasted_iota(jnp.int32, (2 * G, G), 1)
    for t in range(4):
        q = qs[lax.rem(head + 4 - t, 4)]
        limit = jnp.minimum(row + (8 * t + 2 * k) * G, valid - 1)
        top = None
        for m in range(4 * t + 4):
            s = lax.dot_general(
                q, keys[m * 2 * G : (m + 1) * 2 * G], NT, preferred_element_type=F32
            )
            for u in range(2):
                n = 2 * m + u
                part = s[:, u * G : (u + 1) * G]
                if n >= 8 * t:
                    part = jnp.where(lane + n * G <= limit, part, -1e30)
                scores[:, n * G : (n + 1) * G] = part
                top = part if top is None else jnp.maximum(top, part)
        top = jnp.max(top, axis=1, keepdims=True)
        total = None
        for n in range(8 * t + 8):
            part = jnp.exp2((scores[:, n * G : (n + 1) * G] - top) * factor)
            w_ref[2 * t * G : (2 * t + 2) * G, n * G : (n + 1) * G] = part.astype(BF)
            total = part if total is None else total + part
        total = jnp.sum(total, axis=1, keepdims=True)
        total_ref[2 * t * G : (2 * t + 2) * G, :] = jnp.broadcast_to(total, (2 * G, G))


def values_kernel(w_ref, total_ref, v0, v1, v2, v3, msg_ref, vals):
    _, _, k, core = place()
    for d, v_ref in enumerate((v0, v1, v2, v3)):
        row = pl.multiple_of(lax.rem(k + 4 - d, 4) * CH, CH)
        for s in range(NB):
            block = v_ref[s]
            vals[pl.ds(row, CH), s * G : (s + 1) * G] = block
            vals[pl.ds(row + 64, CH), s * G : (s + 1) * G] = block
    lane = lax.broadcasted_iota(jnp.int32, (64, G), 1)
    mine = (lane < 64) != (core == 1)
    for t in range(4):
        n = (8 * t + 8) * G
        rows = slice(2 * t * G, (2 * t + 2) * G)
        out = lax.dot_general(w_ref[rows, 0:n], vals[:, 0:n], NT, preferred_element_type=F32)
        out = out / total_ref[rows, :]
        for c in range(2):
            j = 2 * t + c
            a = out[c * G : c * G + 64]
            b = out[c * G + 64 : (c + 1) * G]
            msg_ref[j, 0:64, :] = jnp.where(mine, a, b).astype(BF)
            col = pl.multiple_of((8 * t + 2 * k + c) * G, G)
            msg_ref[j, 64:128, :] = vals[0:64, pl.ds(col, G)]


def gather_kernel(msg_ref, attended_ref, sum_ref):
    left = lax.broadcasted_iota(jnp.int32, (64, G), 1) < 64
    ones = jnp.ones((8, G), BF)
    sums = jnp.zeros((8, G), F32)
    for h in range(4):
        cols = slice(h * HD, (h + 1) * HD)
        p0 = msg_ref[2 * h, 0:64, :].astype(F32)
        p1 = msg_ref[2 * h + 1, 0:64, :].astype(F32)
        low = jnp.where(left, p0, p1)
        high = pltpu.roll(jnp.where(left, p1, p0), 64, 1)
        both = jnp.concatenate([low, high], axis=0)
        attended_ref[:, cols] = both.astype(BF)
        for part in split(both * both):
            sums += lax.dot_general(ones, part, NT, preferred_element_type=F32)
    sum_ref[...] = sums


def hyena_kernel(msg_ref, hyena_ref):
    for h in range(4):
        block = msg_ref[2 * h : 2 * h + 2, 64:128, :].reshape(G, G).astype(F32)
        hyena_ref[:, h * HD : (h + 1) * HD] = block.T.astype(BF)


def final_kernel(valid_ref, attended_ref, sum_ref, attn_ref):
    valid, own = valid_ref[0], place()[0]
    total = jnp.sum(sum_ref[...], axis=0, keepdims=True)
    norm = jnp.sqrt(total * (1.0 / DW) + 1e-06)
    inv = jnp.broadcast_to(1.0 / norm, (G, G)).T
    row = lax.broadcasted_iota(jnp.int32, (G, G), 0)
    inv = jnp.where(row + own * G < valid, inv, 0.0)
    for h in range(4):
        cols = slice(h * HD, (h + 1) * HD)
        attn_ref[:, cols] = (attended_ref[:, cols].astype(F32) * inv).astype(BF)


def sds(shape, dtype):
    return jax.ShapeDtypeStruct(shape, dtype)


VM = pl.BlockSpec(memory_space=pltpu.MemorySpace.VMEM)
SM = pl.BlockSpec(memory_space=pltpu.MemorySpace.SMEM)
AN = pl.BlockSpec(memory_space=pl.ANY)
HB = pl.BlockSpec(memory_space=pltpu.MemorySpace.HBM)


def call(kernel, out_shape, in_specs, scratch=(), out_specs=None, us=1, vmem=16):
    many = isinstance(out_shape, (tuple, list))
    return pl.pallas_call(
        kernel,
        out_shape=out_shape,
        in_specs=in_specs,
        out_specs=out_specs or ([VM] * len(out_shape) if many else VM),
        scratch_shapes=list(scratch),
        compiler_params=pltpu.CompilerParams(vmem_limit_bytes=vmem << 20),
        cost_estimate=pl.CostEstimate(
            flops=int(us * 10**9), bytes_accessed=int(us * 2 * 10**6), transcendentals=0
        ),
    )


def dma(n):
    return pltpu.SemaphoreType.DMA((n,))


def shards(
    hyena_gate, hyena_key, hyena_value, filter_taps, skip_weight, queries, attn_keys, valid_length
):
    high, low, high_t, low_t, twiddle = (jnp.asarray(t) for t in tables())

    block = pltpu.VMEM((G, 4 * HD), BF)
    msg, *q = call(
        pre_kernel,
        (sds((NB, 96, G), BF),) + (sds((G, HD), BF),) * 4,
        [HB] * 5,
        [block] * 5 + [dma(5)],
        vmem=60,
    )(hyena_key, hyena_value, hyena_gate, attn_keys, queries)
    got = lax.all_to_all(msg, "ctx", 0, 0, tiled=True)
    q = [q[0]] + [lax.ppermute(q[d], "ctx", along_y(d)) for d in (1, 2, 3)]
    q += [lax.ppermute(x, "ctx", CORES) for x in q]
    spec = call(
        taps_kernel,
        sds((NB * CH, 2 * G), F32),
        [HB] + [AN] * 3,
        [
            pltpu.VMEM((SEQ, HD), BF),
            pltpu.VMEM((NB * CH, 2 * G), F32),
            pltpu.VMEM((2, NB, G), F32),
            pltpu.VMEM((2 * G, 2 * G), BF),
            pltpu.VMEM((2 * G, 2 * G), BF),
            dma(7),
        ],
        us=2,
        vmem=50,
    )(filter_taps, twiddle, high, low)
    got_other = lax.ppermute(got, "ctx", CORES)
    values = call(
        conv_kernel,
        sds((NB, CH, G), BF),
        [SM, VM, VM, SM] + [VM] * 5,
        [pltpu.VMEM((NB * CH, 2 * G), F32)],
        us=3,
    )(valid_length, got, spec, skip_weight, twiddle, high, low, high_t, low_t)
    v = [values] + [lax.ppermute(values, "ctx", along_x(d)) for d in (1, 2, 3)]
    weights, totals = call(
        weights_kernel,
        (sds((8 * G, SEQ), BF), sds((8 * G, G), F32)),
        [SM] + [VM] * 8 + [VM] * 2,
        [pltpu.VMEM((4, 2 * G, HD), BF), pltpu.VMEM((SEQ, HD), BF), pltpu.VMEM((2 * G, SEQ), F32)],
        us=4,
    )(valid_length, *q, got, got_other)
    back = call(
        values_kernel,
        sds((8, G, G), BF),
        [VM] * 6,
        [pltpu.VMEM((G, SEQ), BF)],
        us=4,
    )(weights, totals, *v)
    got_back = lax.all_to_all(back, "ctx", 0, 0, tiled=True, axis_index_groups=COLS)
    attended, sums = call(gather_kernel, (sds((G, 4 * HD), BF), sds((8, G), F32)), [VM])(got_back)
    sums = lax.all_to_all(sums, "tp", 0, 0, tiled=True)
    hyena_out = call(hyena_kernel, sds((G, 4 * HD), BF), [VM])(got_back)
    attn_out = call(final_kernel, sds((G, 4 * HD), BF), [SM, VM, VM])(valid_length, attended, sums)
    return hyena_out, attn_out


def solution(mesh):
    in_specs = (
        P("ctx", "tp"),
        P("ctx", "tp"),
        P("ctx", "tp"),
        P(None, "tp"),
        P("tp"),
        P("ctx", "tp"),
        P("ctx", "tp"),
        P(),
    )
    out_specs = (P("ctx", "tp"), P("ctx", "tp"))
    return jax.shard_map(shards, mesh=mesh, in_specs=in_specs, out_specs=out_specs, check_vma=False)
```

```python
import math

import jax
import jax.numpy as jnp
import numpy as np
from jax import lax
from jax.experimental import pallas as pl
from jax.experimental.pallas import tpu as pltpu
from jax.sharding import PartitionSpec as P


HD = 128
DW = 4096
SEQ = 4096
G = 128
NB = SEQ // G
CH = 16
DELTA = 0.25

COLS = [[8 * y + 2 * x + e for y in range(4) for e in range(2)] for x in range(4)]
CORES = [(i, i ^ 1) for i in range(32)]


def along_y(d):
    return [(i, (i + 8 * d) % 32) for i in range(32)]


def along_x(d):
    return [(i, 8 * (i // 8) + (i + 2 * d) % 8) for i in range(32)]


BF = jnp.bfloat16
F32 = jnp.float32
NT = (((1,), (1,)), ((), ()))


def tables():
    b = np.arange(G)
    ang = 2.0 * np.pi * np.outer(b, b) / G
    c, s = np.cos(ang), np.sin(ang)
    fwd = np.block([[c, -s], [s, c]]).astype(np.float32)
    high = fwd.astype(jnp.bfloat16)
    low = (fwd - high.astype(np.float32)).astype(jnp.bfloat16)
    phase = 2.0 * np.pi * np.outer(np.arange(NB) + DELTA, b) / SEQ
    twiddle = np.stack([np.cos(phase), np.sin(phase)]).astype(np.float32)
    return high, low, high.T.copy(), low.T.copy(), twiddle


def cmul_const(z, ang):
    re, im = z
    c, s = math.cos(ang), math.sin(ang)
    if im is None:
        return (re * c, re * s) if abs(s) > 1e-12 else (re, jnp.zeros_like(re))
    if abs(s) < 1e-12:
        return (re, im) if c > 0 else (-re, -im)
    if abs(c) < 1e-12:
        return (-im, re) if s > 0 else (im, -re)
    return (re * c - im * s, re * s + im * c)


def fft(z, sign):
    n = len(z)
    if n == 1:
        return z
    half = n // 2
    up, down = [], []
    for j in range(half):
        (ar, ai), (br, bi) = z[j], z[j + half]
        up.append((ar + br, ai + bi))
        down.append(cmul_const((ar - br, ai - bi), sign * 2.0 * math.pi * j / n))
    even, odd = fft(up, sign), fft(down, sign)
    out = []
    for e, o in zip(even, odd):
        out += [e, o]
    return out


def split(x):
    high = x.astype(BF)
    return high, (x - high.astype(F32)).astype(BF)


def dot3(x, m_high, m_low):
    high, low = split(x)
    return (
        jnp.dot(high, m_high, preferred_element_type=F32)
        + jnp.dot(low, m_high, preferred_element_type=F32)
        + jnp.dot(high, m_low, preferred_element_type=F32)
    )


def spectrum(blocks, tw_ref, mh_ref, ml_ref, buf):
    z = [cmul_const((x, None), -2.0 * math.pi * DELTA * i / NB) for i, x in enumerate(blocks)]
    z = fft(z, -1.0)
    for p, (re, im) in enumerate(z):
        c, s = tw_ref[0, p : p + 1, :], tw_ref[1, p : p + 1, :]
        buf[p * CH : (p + 1) * CH, :G] = re * c + im * s
        buf[p * CH : (p + 1) * CH, G:] = im * c - re * s
    return dot3(buf[...], mh_ref[...], ml_ref[...])


def place():
    own = lax.axis_index("ctx").astype(jnp.int32)
    k = lax.bitwise_and(lax.shift_right_logical(own, 1), 3)
    return own, lax.shift_right_logical(own, 3), k, lax.bitwise_and(own, 1)


def load(pairs, sems):
    copies = [pltpu.make_async_copy(a, b, sems.at[n]) for n, (a, b) in enumerate(pairs)]
    for copy in copies:
        copy.start()
    return copies


def flip(eye, block):
    return lax.dot_general(eye, block, NT, preferred_element_type=F32).astype(BF)


def identity():
    row = lax.broadcasted_iota(jnp.int32, (G, G), 0)
    lane = lax.broadcasted_iota(jnp.int32, (G, G), 1)
    return jnp.where(row == lane, 1.0, 0.0).astype(BF)


def pre_kernel(key_hbm, value_hbm, gate_hbm, attn_hbm, msg_hbm, key, value, gate, attn, msg, sems, done):
    copies = load(
        [(key_hbm, key), (value_hbm, value), (gate_hbm, gate), (attn_hbm, attn)], sems
    )
    eye = identity()
    for copy in copies:
        copy.wait()
    out = []
    for h in range(4):
        cols = slice(h * HD, (h + 1) * HD)
        mixed = flip(eye, (key[:, cols].astype(F32) * value[:, cols].astype(F32)).astype(BF))
        gated = flip(eye, gate[:, cols])
        for c in range(2):
            for k in range(4):
                e = 8 * h + 2 * k + c
                rows = slice(c * 64 + k * CH, c * 64 + (k + 1) * CH)
                msg[e, 0:64, :] = attn[c * 64 : (c + 1) * 64, cols]
                msg[e, 64:80, :] = mixed[rows]
                msg[e, 80:96, :] = gated[rows]
        part = pl.ds(8 * h, 8)
        out += load([(msg.at[part], msg_hbm.at[part])], done.at[pl.ds(h, 1)])
    for copy in out:
        copy.wait()


def query_kernel(own_hbm, other_hbm, q0, q1, q2, q3, own_ref, other_ref, sems):
    copies = load([(own_hbm, own_ref), (other_hbm, other_ref)], sems)
    _, head, _, core = place()
    swap = core == 1
    for copy in copies:
        copy.wait()
    for d, q_ref in enumerate((q0, q1, q2, q3)):
        cols = pl.ds(pl.multiple_of(lax.rem(head + d, 4) * HD, HD), HD)
        own, other = own_ref[:, cols], other_ref[:, cols]
        q_ref[0] = jnp.where(swap, other, own)
        q_ref[1] = jnp.where(swap, own, other)


def taps_kernel(
    taps_hbm, tw_hbm, mh_hbm, ml_hbm, out_ref, taps_ref, buf, tw_ref, mh_ref, ml_ref, sems
):
    _, head, k, core = place()
    col = pl.multiple_of(head * HD, HD)
    parts = 4
    size = SEQ // parts
    copies = load(
        [
            (
                taps_hbm.at[pl.ds(n * size, size), pl.ds(col, HD)],
                taps_ref.at[pl.ds(n * size, size), :],
            )
            for n in range(parts)
        ]
        + [(tw_hbm, tw_ref), (mh_hbm, mh_ref), (ml_hbm, ml_ref)],
        sems,
    )
    first = core * 64 + k * CH
    row = lax.broadcasted_iota(jnp.int32, (CH, G), 0)
    lane = lax.broadcasted_iota(jnp.int32, (CH, G), 1)
    pick = jnp.where(lane == row + first, 1.0, 0.0).astype(BF)
    for copy in copies:
        copy.wait()
    blocks = [
        lax.dot_general(pick, taps_ref[i * G : (i + 1) * G, :], NT, preferred_element_type=F32)
        for i in range(NB)
    ]
    out_ref[...] = spectrum(blocks, tw_ref, mh_ref, ml_ref, buf)


def conv_kernel(
    valid_ref, in_ref, spec_ref, skip_ref, tw_ref, mh_ref, ml_ref, nh_ref, nl_ref, out_ref, buf
):
    valid = valid_ref[0]
    _, head, k, core = place()
    blocks = [in_ref[i, 64:80, :].astype(F32) for i in range(NB)]
    x = spectrum(blocks, tw_ref, mh_ref, ml_ref, buf)
    xr, xi, hr, hi = x[:, :G], x[:, G:], spec_ref[:, :G], spec_ref[:, G:]
    buf[:, :G] = xr * hr - xi * hi
    buf[:, G:] = xr * hi + xi * hr
    buf[...] = dot3(buf[...], nh_ref[...], nl_ref[...])
    z = []
    for p in range(NB):
        re, im = buf[p * CH : (p + 1) * CH, :G], buf[p * CH : (p + 1) * CH, G:]
        c, s = tw_ref[0, p : p + 1, :], tw_ref[1, p : p + 1, :]
        z.append((re * c - im * s, im * c + re * s))
    z = fft(z, 1.0)
    row = lax.broadcasted_iota(jnp.int32, (CH, G), 0)
    lane = lax.broadcasted_iota(jnp.int32, (CH, G), 1)
    skip = jnp.zeros((CH, G), F32)
    for r in range(CH):
        skip = jnp.where(row == r, skip_ref[head * HD + core * 64 + k * CH + r], skip)
    for i, (re, im) in enumerate(z):
        ang = 2.0 * math.pi * DELTA * i / NB
        y = (re * math.cos(ang) - im * math.sin(ang)) * (1.0 / SEQ)
        y = in_ref[i, 80:96, :].astype(F32) * (y + skip * in_ref[i, 64:80, :].astype(F32))
        out_ref[i] = jnp.where(lane + i * G < valid, y, 0.0).astype(BF)


def weights_kernel(valid_ref, *refs):
    q_refs, (own_ref, other_ref, w_ref, total_ref, qs, keys, scores) = refs[:4], refs[4:]
    _, head, k, core = place()
    valid = valid_ref[0]
    swap = core == 1
    for d in range(4):
        qs[d] = q_refs[d][...].reshape(2 * G, HD)
    for s in range(NB):
        own, other = own_ref[s, 0:64], other_ref[s, 0:64]
        keys[s * G : s * G + 64] = jnp.where(swap, other, own)
        keys[s * G + 64 : (s + 1) * G] = jnp.where(swap, own, other)
    factor = math.log2(math.e) / math.sqrt(HD)
    row = lax.broadcasted_iota(jnp.int32, (2 * G, G), 0)
    lane = lax.broadcasted_iota(jnp.int32, (2 * G, G), 1)
    for t in range(4):
        q = qs[lax.rem(head + 4 - t, 4)]
        limit = jnp.minimum(row + (8 * t + 2 * k) * G, valid - 1)
        top = None
        for m in range(4 * t + 4):
            s = lax.dot_general(
                q, keys[m * 2 * G : (m + 1) * 2 * G], NT, preferred_element_type=F32
            )
            for u in range(2):
                n = 2 * m + u
                part = s[:, u * G : (u + 1) * G]
                if n >= 8 * t:
                    part = jnp.where(lane + n * G <= limit, part, -1e30)
                scores[:, n * G : (n + 1) * G] = part
                top = part if top is None else jnp.maximum(top, part)
        top = jnp.max(top, axis=1, keepdims=True)
        total = None
        for n in range(8 * t + 8):
            part = jnp.exp2((scores[:, n * G : (n + 1) * G] - top) * factor)
            w_ref[2 * t * G : (2 * t + 2) * G, n * G : (n + 1) * G] = part.astype(BF)
            total = part if total is None else total + part
        total = jnp.sum(total, axis=1, keepdims=True)
        total_ref[2 * t * G : (2 * t + 2) * G, :] = jnp.broadcast_to(total, (2 * G, G))


def values_kernel(w_ref, total_ref, v0, v1, v2, v3, msg_ref, vals):
    _, _, k, core = place()
    for d, v_ref in enumerate((v0, v1, v2, v3)):
        row = pl.multiple_of(lax.rem(k + 4 - d, 4) * CH, CH)
        for s in range(NB):
            block = v_ref[s]
            vals[pl.ds(row, CH), s * G : (s + 1) * G] = block
            vals[pl.ds(row + 64, CH), s * G : (s + 1) * G] = block
    lane = lax.broadcasted_iota(jnp.int32, (64, G), 1)
    mine = (lane < 64) != (core == 1)
    for t in range(4):
        n = (8 * t + 8) * G
        rows = slice(2 * t * G, (2 * t + 2) * G)
        out = lax.dot_general(w_ref[rows, 0:n], vals[:, 0:n], NT, preferred_element_type=F32)
        out = out / total_ref[rows, :]
        for c in range(2):
            j = 2 * t + c
            a = out[c * G : c * G + 64]
            b = out[c * G + 64 : (c + 1) * G]
            msg_ref[j, 0:64, :] = jnp.where(mine, a, b).astype(BF)
            col = pl.multiple_of((8 * t + 2 * k + c) * G, G)
            msg_ref[j, 64:128, :] = vals[0:64, pl.ds(col, G)]


def gather_kernel(msg_ref, attended_ref, sum_ref):
    left = lax.broadcasted_iota(jnp.int32, (64, G), 1) < 64
    sums = jnp.zeros((G, G), F32)
    for h in range(4):
        p0 = msg_ref[2 * h, 0:64, :].astype(F32)
        p1 = msg_ref[2 * h + 1, 0:64, :].astype(F32)
        low = jnp.where(left, p0, p1)
        high = pltpu.roll(jnp.where(left, p1, p0), 64, 1)
        both = jnp.concatenate([low, high], axis=0)
        attended_ref[:, h * HD : (h + 1) * HD] = both.astype(BF)
        sums += both * both
    sum_ref[...] = jnp.broadcast_to(jnp.sum(sums.T, axis=0, keepdims=True), (8, G))


def hyena_kernel(msg_ref, hyena_ref):
    eye = identity()
    for h in range(4):
        block = msg_ref[2 * h : 2 * h + 2, 64:128, :].reshape(G, G)
        hyena_ref[:, h * HD : (h + 1) * HD] = flip(eye, block)


def final_kernel(valid_ref, attended_ref, sum_ref, attn_ref):
    valid, own = valid_ref[0], place()[0]
    total = jnp.sum(sum_ref[...], axis=0, keepdims=True)
    norm = jnp.sqrt(total * (1.0 / DW) + 1e-06)
    inv = jnp.broadcast_to(1.0 / norm, (G, G)).T
    row = lax.broadcasted_iota(jnp.int32, (G, G), 0)
    inv = jnp.where(row + own * G < valid, inv, 0.0)
    for h in range(4):
        cols = slice(h * HD, (h + 1) * HD)
        attn_ref[:, cols] = (attended_ref[:, cols].astype(F32) * inv).astype(BF)


def sds(shape, dtype):
    return jax.ShapeDtypeStruct(shape, dtype)


VM = pl.BlockSpec(memory_space=pltpu.MemorySpace.VMEM)
SM = pl.BlockSpec(memory_space=pltpu.MemorySpace.SMEM)
AN = pl.BlockSpec(memory_space=pl.ANY)
HB = pl.BlockSpec(memory_space=pltpu.MemorySpace.HBM)


def call(kernel, out_shape, in_specs, scratch=(), out_specs=None, us=1, vmem=16):
    many = isinstance(out_shape, (tuple, list))
    return pl.pallas_call(
        kernel,
        out_shape=out_shape,
        in_specs=in_specs,
        out_specs=out_specs or ([VM] * len(out_shape) if many else VM),
        scratch_shapes=list(scratch),
        compiler_params=pltpu.CompilerParams(vmem_limit_bytes=vmem << 20),
        cost_estimate=pl.CostEstimate(
            flops=int(us * 10**9), bytes_accessed=int(us * 2 * 10**6), transcendentals=0
        ),
    )


QV = 50


def dma(n):
    return pltpu.SemaphoreType.DMA((n,))


def shards(
    hyena_gate, hyena_key, hyena_value, filter_taps, skip_weight, queries, attn_keys, valid_length
):
    high, low, high_t, low_t, twiddle = (jnp.asarray(t) for t in tables())

    block = pltpu.VMEM((G, 4 * HD), BF)
    other_queries = lax.ppermute(queries, "ctx", CORES)
    msg = call(
        pre_kernel,
        sds((NB, 96, G), BF),
        [HB] * 4,
        [block] * 4 + [pltpu.VMEM((NB, 96, G), BF), dma(4), dma(4)],
        out_specs=HB,
        vmem=60,
    )(hyena_key, hyena_value, hyena_gate, attn_keys)
    got = lax.all_to_all(msg, "ctx", 0, 0, tiled=True)
    q = call(
        query_kernel,
        (sds((2, G, HD), BF),) * 4,
        [HB, AN],
        [block, block, dma(2)],
        vmem=QV,
    )(queries, other_queries)
    q = [q[0]] + [lax.ppermute(q[d], "ctx", along_y(d)) for d in (1, 2, 3)]
    spec = call(
        taps_kernel,
        sds((NB * CH, 2 * G), F32),
        [HB] + [AN] * 3,
        [
            pltpu.VMEM((SEQ, HD), BF),
            pltpu.VMEM((NB * CH, 2 * G), F32),
            pltpu.VMEM((2, NB, G), F32),
            pltpu.VMEM((2 * G, 2 * G), BF),
            pltpu.VMEM((2 * G, 2 * G), BF),
            dma(7),
        ],
        us=2,
        vmem=50,
    )(filter_taps, twiddle, high, low)
    got_other = lax.ppermute(got, "ctx", CORES)
    values = call(
        conv_kernel,
        sds((NB, CH, G), BF),
        [SM, VM, VM, SM] + [VM] * 5,
        [pltpu.VMEM((NB * CH, 2 * G), F32)],
        us=3,
    )(valid_length, got, spec, skip_weight, twiddle, high, low, high_t, low_t)
    far = lax.ppermute(values, "ctx", along_x(2))
    near = [lax.ppermute(values, "ctx", along_x(d)) for d in (1, 3)]
    v = [values, near[0], far, near[1]]
    weights, totals = call(
        weights_kernel,
        (sds((8 * G, SEQ), BF), sds((8 * G, G), F32)),
        [SM] + [VM] * 6,
        [pltpu.VMEM((4, 2 * G, HD), BF), pltpu.VMEM((SEQ, HD), BF), pltpu.VMEM((2 * G, SEQ), F32)],
        us=4,
    )(valid_length, *q, got, got_other)
    back = call(
        values_kernel,
        sds((8, G, G), BF),
        [VM] * 6,
        [pltpu.VMEM((G, SEQ), BF)],
        us=4,
    )(weights, totals, *v)
    got_back = lax.all_to_all(back, "ctx", 0, 0, tiled=True, axis_index_groups=COLS)
    attended, sums = call(gather_kernel, (sds((G, 4 * HD), BF), sds((8, G), F32)), [VM])(got_back)
    sums = lax.all_to_all(sums, "tp", 0, 0, tiled=True)
    hyena_out = call(hyena_kernel, sds((G, 4 * HD), BF), [VM])(got_back)
    attn_out = call(final_kernel, sds((G, 4 * HD), BF), [SM, VM, VM])(valid_length, attended, sums)
    return hyena_out, attn_out


def solution(mesh):
    in_specs = (
        P("ctx", "tp"),
        P("ctx", "tp"),
        P("ctx", "tp"),
        P(None, "tp"),
        P("tp"),
        P("ctx", "tp"),
        P("ctx", "tp"),
        P(),
    )
    out_specs = (P("ctx", "tp"), P("ctx", "tp"))
    return jax.shard_map(shards, mesh=mesh, in_specs=in_specs, out_specs=out_specs, check_vma=False)
```

```python
import math

import jax
import jax.numpy as jnp
import numpy as np
from jax import lax
from jax.experimental import pallas as pl
from jax.experimental.pallas import tpu as pltpu
from jax.sharding import PartitionSpec as P


HD = 128
DW = 4096
SEQ = 4096
G = 128
NB = SEQ // G
CH = 16
DELTA = 0.25

CORES = [(i, i ^ 1) for i in range(32)]


def along_y(d):
    return [(i, (i + 8 * d) % 32) for i in range(32)]


def along_x(d):
    return [(i, 8 * (i // 8) + (i + 2 * d) % 8) for i in range(32)]


BF = jnp.bfloat16
F32 = jnp.float32
NT = (((1,), (1,)), ((), ()))


def tables():
    b = np.arange(G)
    ang = 2.0 * np.pi * np.outer(b, b) / G
    c, s = np.cos(ang), np.sin(ang)
    fwd = np.block([[c, -s], [s, c]]).astype(np.float32)
    high = fwd.astype(jnp.bfloat16)
    low = (fwd - high.astype(np.float32)).astype(jnp.bfloat16)
    phase = 2.0 * np.pi * np.outer(np.arange(NB) + DELTA, b) / SEQ
    twiddle = np.stack([np.cos(phase), np.sin(phase)]).astype(np.float32)
    return high, low, high.T.copy(), low.T.copy(), twiddle


def cmul_const(z, ang):
    re, im = z
    c, s = math.cos(ang), math.sin(ang)
    if im is None:
        return (re * c, re * s) if abs(s) > 1e-12 else (re, jnp.zeros_like(re))
    if abs(s) < 1e-12:
        return (re, im) if c > 0 else (-re, -im)
    if abs(c) < 1e-12:
        return (-im, re) if s > 0 else (im, -re)
    return (re * c - im * s, re * s + im * c)


def fft(z, sign):
    n = len(z)
    if n == 1:
        return z
    half = n // 2
    up, down = [], []
    for j in range(half):
        (ar, ai), (br, bi) = z[j], z[j + half]
        up.append((ar + br, ai + bi))
        down.append(cmul_const((ar - br, ai - bi), sign * 2.0 * math.pi * j / n))
    even, odd = fft(up, sign), fft(down, sign)
    out = []
    for e, o in zip(even, odd):
        out += [e, o]
    return out


def split(x):
    high = x.astype(BF)
    return high, (x - high.astype(F32)).astype(BF)


def dot3(x, m_high, m_low):
    high, low = split(x)
    return (
        jnp.dot(high, m_high, preferred_element_type=F32)
        + jnp.dot(low, m_high, preferred_element_type=F32)
        + jnp.dot(high, m_low, preferred_element_type=F32)
    )


def spectrum(blocks, tw_ref, mh_ref, ml_ref, buf):
    z = [cmul_const((x, None), -2.0 * math.pi * DELTA * i / NB) for i, x in enumerate(blocks)]
    z = fft(z, -1.0)
    for p, (re, im) in enumerate(z):
        c, s = tw_ref[0, p : p + 1, :], tw_ref[1, p : p + 1, :]
        buf[p * CH : (p + 1) * CH, :G] = re * c + im * s
        buf[p * CH : (p + 1) * CH, G:] = im * c - re * s
    return dot3(buf[...], mh_ref[...], ml_ref[...])


def place():
    own = lax.axis_index("ctx").astype(jnp.int32)
    k = lax.bitwise_and(lax.shift_right_logical(own, 1), 3)
    return own, lax.shift_right_logical(own, 3), k, lax.bitwise_and(own, 1)


def load(pairs, sems):
    copies = [pltpu.make_async_copy(a, b, sems.at[n]) for n, (a, b) in enumerate(pairs)]
    for copy in copies:
        copy.start()
    return copies


def flip(eye, block):
    return lax.dot_general(eye, block, NT, preferred_element_type=F32).astype(BF)


def identity():
    row = lax.broadcasted_iota(jnp.int32, (G, G), 0)
    lane = lax.broadcasted_iota(jnp.int32, (G, G), 1)
    return jnp.where(row == lane, 1.0, 0.0).astype(BF)


def pre_kernel(key_hbm, value_hbm, gate_hbm, attn_hbm, msg_hbm, key, value, gate, attn, msg, sems, done):
    copies = load(
        [(key_hbm, key), (value_hbm, value), (gate_hbm, gate), (attn_hbm, attn)], sems
    )
    eye = identity()
    for copy in copies:
        copy.wait()
    out = []
    for h in range(4):
        cols = slice(h * HD, (h + 1) * HD)
        mixed = flip(eye, (key[:, cols].astype(F32) * value[:, cols].astype(F32)).astype(BF))
        gated = flip(eye, gate[:, cols])
        for c in range(2):
            for k in range(4):
                e = 8 * h + 2 * k + c
                rows = slice(c * 64 + k * CH, c * 64 + (k + 1) * CH)
                msg[e, 0:64, :] = attn[c * 64 : (c + 1) * 64, cols]
                msg[e, 64:80, :] = mixed[rows]
                msg[e, 80:96, :] = gated[rows]
        part = pl.ds(8 * h, 8)
        out += load([(msg.at[part], msg_hbm.at[part])], done.at[pl.ds(h, 1)])
    for copy in out:
        copy.wait()


def query_kernel(own_hbm, q0, q1, q2, q3, own_ref, sems):
    copies = load([(own_hbm, own_ref)], sems)
    head = place()[1]
    copies[0].wait()
    for d, q_ref in enumerate((q0, q1, q2, q3)):
        cols = pl.ds(pl.multiple_of(lax.rem(head + d, 4) * HD, HD), HD)
        q_ref[...] = own_ref[:, cols]


def taps_kernel(
    taps_hbm, tw_hbm, mh_hbm, ml_hbm, out_ref, taps_ref, buf, tw_ref, mh_ref, ml_ref, sems
):
    _, head, k, core = place()
    col = pl.multiple_of(head * HD, HD)
    parts = 4
    size = SEQ // parts
    copies = load(
        [
            (
                taps_hbm.at[pl.ds(n * size, size), pl.ds(col, HD)],
                taps_ref.at[pl.ds(n * size, size), :],
            )
            for n in range(parts)
        ]
        + [(tw_hbm, tw_ref), (mh_hbm, mh_ref), (ml_hbm, ml_ref)],
        sems,
    )
    first = core * 64 + k * CH
    row = lax.broadcasted_iota(jnp.int32, (CH, G), 0)
    lane = lax.broadcasted_iota(jnp.int32, (CH, G), 1)
    pick = jnp.where(lane == row + first, 1.0, 0.0).astype(BF)
    for copy in copies:
        copy.wait()
    blocks = [
        lax.dot_general(pick, taps_ref[i * G : (i + 1) * G, :], NT, preferred_element_type=F32)
        for i in range(NB)
    ]
    out_ref[...] = spectrum(blocks, tw_ref, mh_ref, ml_ref, buf)


def conv_kernel(
    valid_ref, in_ref, spec_ref, skip_ref, tw_ref, mh_ref, ml_ref, nh_ref, nl_ref, out_ref, buf
):
    valid = valid_ref[0]
    _, head, k, core = place()
    blocks = [in_ref[i, 64:80, :].astype(F32) for i in range(NB)]
    x = spectrum(blocks, tw_ref, mh_ref, ml_ref, buf)
    xr, xi, hr, hi = x[:, :G], x[:, G:], spec_ref[:, :G], spec_ref[:, G:]
    buf[:, :G] = xr * hr - xi * hi
    buf[:, G:] = xr * hi + xi * hr
    buf[...] = dot3(buf[...], nh_ref[...], nl_ref[...])
    z = []
    for p in range(NB):
        re, im = buf[p * CH : (p + 1) * CH, :G], buf[p * CH : (p + 1) * CH, G:]
        c, s = tw_ref[0, p : p + 1, :], tw_ref[1, p : p + 1, :]
        z.append((re * c - im * s, im * c + re * s))
    z = fft(z, 1.0)
    row = lax.broadcasted_iota(jnp.int32, (CH, G), 0)
    lane = lax.broadcasted_iota(jnp.int32, (CH, G), 1)
    skip = jnp.zeros((CH, G), F32)
    for r in range(CH):
        skip = jnp.where(row == r, skip_ref[head * HD + core * 64 + k * CH + r], skip)
    for i, (re, im) in enumerate(z):
        ang = 2.0 * math.pi * DELTA * i / NB
        y = (re * math.cos(ang) - im * math.sin(ang)) * (1.0 / SEQ)
        y = in_ref[i, 80:96, :].astype(F32) * (y + skip * in_ref[i, 64:80, :].astype(F32))
        out_ref[i] = jnp.where(lane + i * G < valid, y, 0.0).astype(BF)


def weights_kernel(valid_ref, *refs):
    q_refs, (own_ref, other_ref, w_ref, inverse_ref, qs, keys, scores) = refs[:4], refs[4:]
    _, head, k, core = place()
    last = valid_ref[0] - 1
    swap = core == 1
    for d in range(4):
        row = pl.multiple_of(lax.rem(head + 4 - d, 4) * G, G)
        qs[pl.ds(row, G), :] = q_refs[d][...]
    for s in range(NB):
        own, other = own_ref[s, 0:64], other_ref[s, 0:64]
        keys[s * G : s * G + 64] = jnp.where(swap, other, own)
        keys[s * G + 64 : (s + 1) * G] = jnp.where(swap, own, other)
    for m in range(16):
        low = m // 4 * G
        s = lax.dot_general(
            qs[low:, :], keys[m * 2 * G : (m + 1) * 2 * G], NT, preferred_element_type=F32
        )
        scores[low:, m * 2 * G : (m + 1) * 2 * G] = s
    factor = math.log2(math.e) / math.sqrt(HD)
    row = lax.broadcasted_iota(jnp.int32, (G, G), 0)
    lane = lax.broadcasted_iota(jnp.int32, (G, G), 1)
    for t in range(4):
        rows = slice(t * G, (t + 1) * G)
        limit = jnp.minimum(row + (8 * t + 2 * k + core) * G, last)

        def part(n):
            block = scores[rows, n * G : (n + 1) * G]
            return jnp.where(lane + n * G <= limit, block, -1e30) if n >= 8 * t else block

        top = part(0)
        for n in range(1, 8 * t + 8):
            top = jnp.maximum(top, part(n))
        top = jnp.max(top, axis=1, keepdims=True)
        total = None
        for n in range(8 * t + 8):
            w = jnp.exp2((part(n) - top) * factor)
            w_ref[rows, n * G : (n + 1) * G] = w.astype(BF)
            total = w if total is None else total + w
        total = jnp.sum(total, axis=1, keepdims=True)
        inverse_ref[rows, :] = jnp.broadcast_to(1.0 / total, (G, G))


def values_kernel(w_ref, inverse_ref, *refs):
    v_refs, out_refs, (vals, acc) = refs[:8], refs[8:12], refs[12:]
    _, head, k, core = place()
    for d, v_ref in enumerate(v_refs):
        side = core if d < 4 else 1 - core
        row = pl.multiple_of(side * 64 + lax.rem(k + 4 - d % 4, 4) * CH, CH)
        for s in range(NB):
            vals[pl.ds(row, CH), s * G : (s + 1) * G] = v_ref[s]
    for t in range(4):
        span = slice(8 * t * G, (8 * t + 8) * G)
        part = lax.dot_general(w_ref[t * G :, span], vals[:, span], NT, preferred_element_type=F32)
        if t == 0:
            acc[...] = part
        else:
            acc[t * G :, :] += part
    for d in range(4):
        t = lax.rem(head + d, 4)
        rows = pl.ds(pl.multiple_of(t * G, G), G)
        out_refs[d][0:G] = (acc[rows, :] * inverse_ref[rows, :]).astype(BF)
        col = pl.multiple_of((8 * t + 2 * k + core) * G, G)
        out_refs[d][G : 2 * G] = vals[:, pl.ds(col, G)]


def gather_kernel(a0, a1, a2, a3, attended_ref, sum_ref):
    head = place()[1]
    sums = jnp.zeros((G, G), F32)
    for d, a_ref in enumerate((a0, a1, a2, a3)):
        cols = pl.ds(pl.multiple_of(lax.rem(head + 4 - d, 4) * HD, HD), HD)
        block = a_ref[0:G]
        attended_ref[:, cols] = block
        sums += block.astype(F32) * block.astype(F32)
    sum_ref[...] = jnp.broadcast_to(jnp.sum(sums.T, axis=0, keepdims=True), (8, G))


def hyena_kernel(h0, h1, h2, h3, hyena_ref):
    eye = identity()
    head = place()[1]
    for d, h_ref in enumerate((h0, h1, h2, h3)):
        cols = pl.ds(pl.multiple_of(lax.rem(head + 4 - d, 4) * HD, HD), HD)
        hyena_ref[:, cols] = flip(eye, h_ref[G : 2 * G])


def final_kernel(valid_ref, attended_ref, sum_ref, attn_ref):
    valid, own = valid_ref[0], place()[0]
    total = jnp.sum(sum_ref[...], axis=0, keepdims=True)
    norm = jnp.sqrt(total * (1.0 / DW) + 1e-06)
    inv = jnp.broadcast_to(1.0 / norm, (G, G)).T
    row = lax.broadcasted_iota(jnp.int32, (G, G), 0)
    inv = jnp.where(row + own * G < valid, inv, 0.0)
    for h in range(4):
        cols = slice(h * HD, (h + 1) * HD)
        attn_ref[:, cols] = (attended_ref[:, cols].astype(F32) * inv).astype(BF)


def sds(shape, dtype):
    return jax.ShapeDtypeStruct(shape, dtype)


VM = pl.BlockSpec(memory_space=pltpu.MemorySpace.VMEM)
SM = pl.BlockSpec(memory_space=pltpu.MemorySpace.SMEM)
AN = pl.BlockSpec(memory_space=pl.ANY)
HB = pl.BlockSpec(memory_space=pltpu.MemorySpace.HBM)


def call(kernel, out_shape, in_specs, scratch=(), out_specs=None, us=1, vmem=16):
    many = isinstance(out_shape, (tuple, list))
    return pl.pallas_call(
        kernel,
        out_shape=out_shape,
        in_specs=in_specs,
        out_specs=out_specs or ([VM] * len(out_shape) if many else VM),
        scratch_shapes=list(scratch),
        compiler_params=pltpu.CompilerParams(vmem_limit_bytes=vmem << 20),
        cost_estimate=pl.CostEstimate(
            flops=int(us * 10**9), bytes_accessed=int(us * 2 * 10**6), transcendentals=0
        ),
    )


QV = 50


def dma(n):
    return pltpu.SemaphoreType.DMA((n,))


def shards(
    hyena_gate, hyena_key, hyena_value, filter_taps, skip_weight, queries, attn_keys, valid_length
):
    high, low, high_t, low_t, twiddle = (jnp.asarray(t) for t in tables())

    block = pltpu.VMEM((G, 4 * HD), BF)
    msg = call(
        pre_kernel,
        sds((NB, 96, G), BF),
        [HB] * 4,
        [block] * 4 + [pltpu.VMEM((NB, 96, G), BF), dma(4), dma(4)],
        out_specs=HB,
        vmem=60,
    )(hyena_key, hyena_value, hyena_gate, attn_keys)
    got = lax.all_to_all(msg, "ctx", 0, 0, tiled=True)
    q = call(
        query_kernel,
        (sds((G, HD), BF),) * 4,
        [HB],
        [block, dma(1)],
        vmem=QV,
    )(queries)
    q = [q[0]] + [lax.ppermute(q[d], "ctx", along_y(d)) for d in (1, 2, 3)]
    spec = call(
        taps_kernel,
        sds((NB * CH, 2 * G), F32),
        [HB] + [AN] * 3,
        [
            pltpu.VMEM((SEQ, HD), BF),
            pltpu.VMEM((NB * CH, 2 * G), F32),
            pltpu.VMEM((2, NB, G), F32),
            pltpu.VMEM((2 * G, 2 * G), BF),
            pltpu.VMEM((2 * G, 2 * G), BF),
            dma(7),
        ],
        us=2,
        vmem=50,
    )(filter_taps, twiddle, high, low)
    got_other = lax.ppermute(got, "ctx", CORES)
    values = call(
        conv_kernel,
        sds((NB, CH, G), BF),
        [SM, VM, VM, SM] + [VM] * 5,
        [pltpu.VMEM((NB * CH, 2 * G), F32)],
        us=3,
    )(valid_length, got, spec, skip_weight, twiddle, high, low, high_t, low_t)
    far = lax.ppermute(values, "ctx", along_x(2))
    near = [lax.ppermute(values, "ctx", along_x(d)) for d in (1, 3)]
    v = [values, near[0], far, near[1]]
    v += [lax.ppermute(x, "ctx", CORES) for x in v]
    weights, inverses = call(
        weights_kernel,
        (sds((4 * G, SEQ), BF), sds((4 * G, G), F32)),
        [SM] + [VM] * 6,
        [pltpu.VMEM((4 * G, HD), BF), pltpu.VMEM((SEQ, HD), BF), pltpu.VMEM((4 * G, SEQ), F32)],
        us=2,
    )(valid_length, *q, got, got_other)
    blocks = call(
        values_kernel,
        (sds((2 * G, G), BF),) * 4,
        [VM] * 10,
        [pltpu.VMEM((G, SEQ), BF), pltpu.VMEM((4 * G, G), F32)],
        us=1,
    )(weights, inverses, *v)
    back = [blocks[0]] + [lax.ppermute(blocks[d], "ctx", along_y(d)) for d in (2, 1, 3)]
    back = [back[0], back[2], back[1], back[3]]
    attended, sums = call(gather_kernel, (sds((G, 4 * HD), BF), sds((8, G), F32)), [VM] * 4)(*back)
    sums = lax.all_to_all(sums, "tp", 0, 0, tiled=True)
    hyena_out = call(hyena_kernel, sds((G, 4 * HD), BF), [VM] * 4)(*back)
    attn_out = call(final_kernel, sds((G, 4 * HD), BF), [SM, VM, VM])(valid_length, attended, sums)
    return hyena_out, attn_out


def solution(mesh):
    in_specs = (
        P("ctx", "tp"),
        P("ctx", "tp"),
        P("ctx", "tp"),
        P(None, "tp"),
        P("tp"),
        P("ctx", "tp"),
        P("ctx", "tp"),
        P(),
    )
    out_specs = (P("ctx", "tp"), P("ctx", "tp"))
    return jax.shard_map(shards, mesh=mesh, in_specs=in_specs, out_specs=out_specs, check_vma=False)
```

```python
import math

import jax
import jax.numpy as jnp
import numpy as np
from jax import lax
from jax.experimental import pallas as pl
from jax.experimental.pallas import tpu as pltpu
from jax.sharding import PartitionSpec as P


HD = 128
DW = 4096
SEQ = 4096
G = 128
NB = SEQ // G
CH = 16
DELTA = 0.25

CORES = [(i, i ^ 1) for i in range(32)]


def along_y(d):
    return [(i, (i + 8 * d) % 32) for i in range(32)]


def along_x(d):
    return [(i, 8 * (i // 8) + (i + 2 * d) % 8) for i in range(32)]


BF = jnp.bfloat16
F32 = jnp.float32
NT = (((1,), (1,)), ((), ()))


def tables():
    b = np.arange(G)
    ang = 2.0 * np.pi * np.outer(b, b) / G
    c, s = np.cos(ang), np.sin(ang)
    fwd = np.block([[c, -s], [s, c]]).astype(np.float32)
    high = fwd.astype(jnp.bfloat16)
    low = (fwd - high.astype(np.float32)).astype(jnp.bfloat16)
    phase = 2.0 * np.pi * np.outer(np.arange(NB) + DELTA, b) / SEQ
    twiddle = np.stack([np.cos(phase), np.sin(phase)]).astype(np.float32)
    return high, low, high.T.copy(), low.T.copy(), twiddle


def cmul_const(z, ang):
    re, im = z
    c, s = math.cos(ang), math.sin(ang)
    if im is None:
        return (re * c, re * s) if abs(s) > 1e-12 else (re, jnp.zeros_like(re))
    if abs(s) < 1e-12:
        return (re, im) if c > 0 else (-re, -im)
    if abs(c) < 1e-12:
        return (-im, re) if s > 0 else (im, -re)
    return (re * c - im * s, re * s + im * c)


def fft(z, sign):
    n = len(z)
    if n == 1:
        return z
    half = n // 2
    up, down = [], []
    for j in range(half):
        (ar, ai), (br, bi) = z[j], z[j + half]
        up.append((ar + br, ai + bi))
        down.append(cmul_const((ar - br, ai - bi), sign * 2.0 * math.pi * j / n))
    even, odd = fft(up, sign), fft(down, sign)
    out = []
    for e, o in zip(even, odd):
        out += [e, o]
    return out


def split(x):
    high = x.astype(BF)
    return high, (x - high.astype(F32)).astype(BF)


def dot3(x, m_high, m_low):
    high, low = split(x)
    return (
        jnp.dot(high, m_high, preferred_element_type=F32)
        + jnp.dot(low, m_high, preferred_element_type=F32)
        + jnp.dot(high, m_low, preferred_element_type=F32)
    )


def spectrum(blocks, tw_ref, mh_ref, ml_ref, buf):
    z = [cmul_const((x, None), -2.0 * math.pi * DELTA * i / NB) for i, x in enumerate(blocks)]
    z = fft(z, -1.0)
    for p, (re, im) in enumerate(z):
        c, s = tw_ref[0, p : p + 1, :], tw_ref[1, p : p + 1, :]
        buf[p * CH : (p + 1) * CH, :G] = re * c + im * s
        buf[p * CH : (p + 1) * CH, G:] = im * c - re * s
    return dot3(buf[...], mh_ref[...], ml_ref[...])


def place():
    own = lax.axis_index("ctx").astype(jnp.int32)
    k = lax.bitwise_and(lax.shift_right_logical(own, 1), 3)
    return own, lax.shift_right_logical(own, 3), k, lax.bitwise_and(own, 1)


def load(pairs, sems):
    copies = [pltpu.make_async_copy(a, b, sems.at[n]) for n, (a, b) in enumerate(pairs)]
    for copy in copies:
        copy.start()
    return copies


def flip(eye, block):
    return lax.dot_general(eye, block, NT, preferred_element_type=F32).astype(BF)


def identity():
    row = lax.broadcasted_iota(jnp.int32, (G, G), 0)
    lane = lax.broadcasted_iota(jnp.int32, (G, G), 1)
    return jnp.where(row == lane, 1.0, 0.0).astype(BF)


def pre_kernel(key_hbm, value_hbm, gate_hbm, msg_hbm, key, value, gate, msg, sems, done):
    copies = load(
        [(key_hbm, key), (value_hbm, value), (gate_hbm, gate)], sems
    )
    eye = identity()
    for copy in copies:
        copy.wait()
    out = []
    for h in range(4):
        cols = slice(h * HD, (h + 1) * HD)
        mixed = flip(eye, (key[:, cols].astype(F32) * value[:, cols].astype(F32)).astype(BF))
        gated = flip(eye, gate[:, cols])
        for c in range(2):
            for k in range(4):
                e = 8 * h + 2 * k + c
                rows = slice(c * 64 + k * CH, c * 64 + (k + 1) * CH)
                msg[e, 0:16, :] = mixed[rows]
                msg[e, 16:32, :] = gated[rows]
        part = pl.ds(8 * h, 8)
        out += load([(msg.at[part], msg_hbm.at[part])], done.at[pl.ds(h, 1)])
    for copy in out:
        copy.wait()


def pack_kernel(q_ref, k0, k1, k2, k3, o0, o1, o2, o3):
    _, head, k, _ = place()
    for d, out in enumerate((o0, o1, o2, o3)):
        cols = pl.ds(pl.multiple_of(lax.rem(head + d, 4) * HD, HD), HD)
        out[4] = q_ref[:, cols]
        for x, keys in enumerate((k0, k1, k2, k3)):
            out[lax.rem(k + 4 - x, 4)] = keys[:, cols]


def taps_kernel(
    taps_hbm, tw_hbm, mh_hbm, ml_hbm, out_ref, taps_ref, buf, tw_ref, mh_ref, ml_ref, sems
):
    _, head, k, core = place()
    col = pl.multiple_of(head * HD, HD)
    parts = 4
    size = SEQ // parts
    copies = load(
        [
            (
                taps_hbm.at[pl.ds(n * size, size), pl.ds(col, HD)],
                taps_ref.at[pl.ds(n * size, size), :],
            )
            for n in range(parts)
        ]
        + [(tw_hbm, tw_ref), (mh_hbm, mh_ref), (ml_hbm, ml_ref)],
        sems,
    )
    first = core * 64 + k * CH
    row = lax.broadcasted_iota(jnp.int32, (CH, G), 0)
    lane = lax.broadcasted_iota(jnp.int32, (CH, G), 1)
    pick = jnp.where(lane == row + first, 1.0, 0.0).astype(BF)
    for copy in copies:
        copy.wait()
    blocks = [
        lax.dot_general(pick, taps_ref[i * G : (i + 1) * G, :], NT, preferred_element_type=F32)
        for i in range(NB)
    ]
    out_ref[...] = spectrum(blocks, tw_ref, mh_ref, ml_ref, buf)


def conv_kernel(
    valid_ref, in_ref, spec_ref, skip_ref, tw_ref, mh_ref, ml_ref, nh_ref, nl_ref, out_ref, buf
):
    valid = valid_ref[0]
    _, head, k, core = place()
    blocks = [in_ref[i, 0:16, :].astype(F32) for i in range(NB)]
    x = spectrum(blocks, tw_ref, mh_ref, ml_ref, buf)
    xr, xi, hr, hi = x[:, :G], x[:, G:], spec_ref[:, :G], spec_ref[:, G:]
    buf[:, :G] = xr * hr - xi * hi
    buf[:, G:] = xr * hi + xi * hr
    buf[...] = dot3(buf[...], nh_ref[...], nl_ref[...])
    z = []
    for p in range(NB):
        re, im = buf[p * CH : (p + 1) * CH, :G], buf[p * CH : (p + 1) * CH, G:]
        c, s = tw_ref[0, p : p + 1, :], tw_ref[1, p : p + 1, :]
        z.append((re * c - im * s, im * c + re * s))
    z = fft(z, 1.0)
    row = lax.broadcasted_iota(jnp.int32, (CH, G), 0)
    lane = lax.broadcasted_iota(jnp.int32, (CH, G), 1)
    skip = jnp.zeros((CH, G), F32)
    for r in range(CH):
        skip = jnp.where(row == r, skip_ref[head * HD + core * 64 + k * CH + r], skip)
    for i, (re, im) in enumerate(z):
        ang = 2.0 * math.pi * DELTA * i / NB
        y = (re * math.cos(ang) - im * math.sin(ang)) * (1.0 / SEQ)
        y = in_ref[i, 16:32, :].astype(F32) * (y + skip * in_ref[i, 0:16, :].astype(F32))
        out_ref[i] = jnp.where(lane + i * G < valid, y, 0.0).astype(BF)


def weights_kernel(valid_ref, *refs):
    own_refs, other_refs, (w_ref, inverse_ref, qs, keys, scores) = refs[:4], refs[4:8], refs[8:]
    _, head, k, core = place()
    last = valid_ref[0] - 1
    for d in range(4):
        y = lax.rem(head + 4 - d, 4)
        qs[pl.ds(pl.multiple_of(y * G, G), G), :] = own_refs[d][4]
        for x in range(4):
            own = pl.multiple_of((8 * y + 2 * x + core) * G, G)
            other = pl.multiple_of((8 * y + 2 * x + 1 - core) * G, G)
            keys[pl.ds(own, G), :] = own_refs[d][x]
            keys[pl.ds(other, G), :] = other_refs[d][x]
    for m in range(16):
        low = m // 4 * G
        s = lax.dot_general(
            qs[low:, :], keys[m * 2 * G : (m + 1) * 2 * G], NT, preferred_element_type=F32
        )
        scores[low:, m * 2 * G : (m + 1) * 2 * G] = s
    factor = math.log2(math.e) / math.sqrt(HD)
    row = lax.broadcasted_iota(jnp.int32, (G, G), 0)
    lane = lax.broadcasted_iota(jnp.int32, (G, G), 1)
    for t in range(4):
        rows = slice(t * G, (t + 1) * G)
        limit = jnp.minimum(row + (8 * t + 2 * k + core) * G, last)

        def part(n):
            block = scores[rows, n * G : (n + 1) * G]
            return jnp.where(lane + n * G <= limit, block, -1e30) if n >= 8 * t else block

        top = part(0)
        for n in range(1, 8 * t + 8):
            top = jnp.maximum(top, part(n))
        top = jnp.max(top, axis=1, keepdims=True)
        total = None
        for n in range(8 * t + 8):
            w = jnp.exp2((part(n) - top) * factor)
            w_ref[rows, n * G : (n + 1) * G] = w.astype(BF)
            total = w if total is None else total + w
        total = jnp.sum(total, axis=1, keepdims=True)
        inverse_ref[rows, :] = jnp.broadcast_to(1.0 / total, (G, G))


def values_kernel(w_ref, inverse_ref, *refs):
    v_refs, out_refs, (vals, acc) = refs[:8], refs[8:12], refs[12:]
    _, head, k, core = place()
    for d, v_ref in enumerate(v_refs):
        side = core if d < 4 else 1 - core
        row = pl.multiple_of(side * 64 + lax.rem(k + 4 - d % 4, 4) * CH, CH)
        for s in range(NB):
            vals[pl.ds(row, CH), s * G : (s + 1) * G] = v_ref[s]
    for t in range(4):
        span = slice(8 * t * G, (8 * t + 8) * G)
        part = lax.dot_general(w_ref[t * G :, span], vals[:, span], NT, preferred_element_type=F32)
        if t == 0:
            acc[...] = part
        else:
            acc[t * G :, :] += part
    for d in range(4):
        t = lax.rem(head + d, 4)
        rows = pl.ds(pl.multiple_of(t * G, G), G)
        out_refs[d][0:G] = (acc[rows, :] * inverse_ref[rows, :]).astype(BF)
        col = pl.multiple_of((8 * t + 2 * k + core) * G, G)
        out_refs[d][G : 2 * G] = vals[:, pl.ds(col, G)]


def gather_kernel(a0, a1, a2, a3, attended_ref, sum_ref):
    head = place()[1]
    sums = jnp.zeros((G, G), F32)
    for d, a_ref in enumerate((a0, a1, a2, a3)):
        cols = pl.ds(pl.multiple_of(lax.rem(head + 4 - d, 4) * HD, HD), HD)
        block = a_ref[0:G]
        attended_ref[:, cols] = block
        sums += block.astype(F32) * block.astype(F32)
    sum_ref[...] = jnp.broadcast_to(jnp.sum(sums.T, axis=0, keepdims=True), (8, G))


def hyena_kernel(h0, h1, h2, h3, hyena_ref):
    eye = identity()
    head = place()[1]
    for d, h_ref in enumerate((h0, h1, h2, h3)):
        cols = pl.ds(pl.multiple_of(lax.rem(head + 4 - d, 4) * HD, HD), HD)
        hyena_ref[:, cols] = flip(eye, h_ref[G : 2 * G])


def final_kernel(valid_ref, attended_ref, sum_ref, attn_ref):
    valid, own = valid_ref[0], place()[0]
    total = jnp.sum(sum_ref[...], axis=0, keepdims=True)
    norm = jnp.sqrt(total * (1.0 / DW) + 1e-06)
    inv = jnp.broadcast_to(1.0 / norm, (G, G)).T
    row = lax.broadcasted_iota(jnp.int32, (G, G), 0)
    inv = jnp.where(row + own * G < valid, inv, 0.0)
    for h in range(4):
        cols = slice(h * HD, (h + 1) * HD)
        attn_ref[:, cols] = (attended_ref[:, cols].astype(F32) * inv).astype(BF)


def sds(shape, dtype):
    return jax.ShapeDtypeStruct(shape, dtype)


VM = pl.BlockSpec(memory_space=pltpu.MemorySpace.VMEM)
SM = pl.BlockSpec(memory_space=pltpu.MemorySpace.SMEM)
AN = pl.BlockSpec(memory_space=pl.ANY)
HB = pl.BlockSpec(memory_space=pltpu.MemorySpace.HBM)


def call(kernel, out_shape, in_specs, scratch=(), out_specs=None, us=1, vmem=16):
    many = isinstance(out_shape, (tuple, list))
    return pl.pallas_call(
        kernel,
        out_shape=out_shape,
        in_specs=in_specs,
        out_specs=out_specs or ([VM] * len(out_shape) if many else VM),
        scratch_shapes=list(scratch),
        compiler_params=pltpu.CompilerParams(vmem_limit_bytes=vmem << 20),
        cost_estimate=pl.CostEstimate(
            flops=int(us * 10**9), bytes_accessed=int(us * 2 * 10**6), transcendentals=0
        ),
    )


QV = 50


def dma(n):
    return pltpu.SemaphoreType.DMA((n,))


def shards(
    hyena_gate, hyena_key, hyena_value, filter_taps, skip_weight, queries, attn_keys, valid_length
):
    high, low, high_t, low_t, twiddle = (jnp.asarray(t) for t in tables())

    block = pltpu.VMEM((G, 4 * HD), BF)
    spread = [attn_keys]
    spread += [lax.ppermute(attn_keys, "ctx", along_x(d)) for d in (1, 2, 3)]
    msg = call(
        pre_kernel,
        sds((NB, 2 * CH, G), BF),
        [HB] * 3,
        [block] * 3 + [pltpu.VMEM((NB, 2 * CH, G), BF), dma(3), dma(4)],
        out_specs=HB,
        vmem=60,
    )(hyena_key, hyena_value, hyena_gate)
    got = lax.all_to_all(msg, "ctx", 0, 0, tiled=True)
    packs = call(pack_kernel, (sds((5, G, HD), BF),) * 4, [VM] * 5, vmem=QV)(queries, *spread)
    packs = [packs[0]] + [lax.ppermute(packs[d], "ctx", along_y(d)) for d in (1, 2, 3)]
    spec = call(
        taps_kernel,
        sds((NB * CH, 2 * G), F32),
        [HB] + [AN] * 3,
        [
            pltpu.VMEM((SEQ, HD), BF),
            pltpu.VMEM((NB * CH, 2 * G), F32),
            pltpu.VMEM((2, NB, G), F32),
            pltpu.VMEM((2 * G, 2 * G), BF),
            pltpu.VMEM((2 * G, 2 * G), BF),
            dma(7),
        ],
        us=2,
        vmem=50,
    )(filter_taps, twiddle, high, low)
    others = [lax.ppermute(x, "ctx", CORES) for x in packs]
    values = call(
        conv_kernel,
        sds((NB, CH, G), BF),
        [SM, VM, VM, SM] + [VM] * 5,
        [pltpu.VMEM((NB * CH, 2 * G), F32)],
        us=3,
    )(valid_length, got, spec, skip_weight, twiddle, high, low, high_t, low_t)
    far = lax.ppermute(values, "ctx", along_x(2))
    near = [lax.ppermute(values, "ctx", along_x(d)) for d in (1, 3)]
    v = [values, near[0], far, near[1]]
    v += [lax.ppermute(x, "ctx", CORES) for x in v]
    weights, inverses = call(
        weights_kernel,
        (sds((4 * G, SEQ), BF), sds((4 * G, G), F32)),
        [SM] + [VM] * 8,
        [pltpu.VMEM((4 * G, HD), BF), pltpu.VMEM((SEQ, HD), BF), pltpu.VMEM((4 * G, SEQ), F32)],
        us=2,
    )(valid_length, *packs, *others)
    blocks = call(
        values_kernel,
        (sds((2 * G, G), BF),) * 4,
        [VM] * 10,
        [pltpu.VMEM((G, SEQ), BF), pltpu.VMEM((4 * G, G), F32)],
        us=1,
    )(weights, inverses, *v)
    back_far = lax.ppermute(blocks[2], "ctx", along_y(2))
    back_near = [lax.ppermute(blocks[d], "ctx", along_y(d)) for d in (1, 3)]
    back = [blocks[0], back_near[0], back_far, back_near[1]]
    attended, sums = call(gather_kernel, (sds((G, 4 * HD), BF), sds((8, G), F32)), [VM] * 4)(*back)
    sums = lax.all_to_all(sums, "tp", 0, 0, tiled=True)
    hyena_out = call(hyena_kernel, sds((G, 4 * HD), BF), [VM] * 4)(*back)
    attn_out = call(final_kernel, sds((G, 4 * HD), BF), [SM, VM, VM])(valid_length, attended, sums)
    return hyena_out, attn_out


def solution(mesh):
    in_specs = (
        P("ctx", "tp"),
        P("ctx", "tp"),
        P("ctx", "tp"),
        P(None, "tp"),
        P("tp"),
        P("ctx", "tp"),
        P("ctx", "tp"),
        P(),
    )
    out_specs = (P("ctx", "tp"), P("ctx", "tp"))
    return jax.shard_map(shards, mesh=mesh, in_specs=in_specs, out_specs=out_specs, check_vma=False)
```
